128 devices in a mesh: dp: 2 (over z_hi), tile: 64 (over x, z_lo, y, core).
Axes of the slice: x: 4, y: 4, z: 4 (z_hi: 2, z_lo: 2; z = z_hi * 2 + z_lo), core: 2. Of those that a mesh axis runs over, the one named last changes fastest.
Arguments:
- inputs: bfloat16 [2, 1024, 8, 8, 128], P('dp', 'tile'), may hold values from -6 to 6
- cotangent: bfloat16 [2, 1024, 4, 4, 128], P('dp', 'tile'), may hold values from -6 to 6
- w_first: bfloat16 [1152, 128], replicated, may hold values from -0.1875 to 0.1875
- w_second: bfloat16 [1152, 128], replicated, may hold values from -0.1875 to 0.1875
- w_down: bfloat16 [512, 128], replicated, may hold values from -0.25 to 0.25
- edge_owner: int32 [1024, 4], replicated, may hold values from 0 to 63, all different within a row; in each aligned block of 16 rows (0 to 15, 16 to 31, ...) at most 2 rows name the same one
- corner_owner: int32 [1024, 4], replicated, may hold values from 0 to 63, all different within a row; in each aligned block of 16 rows (0 to 15, 16 to 31, ...) at most 2 rows name the same one
- neighbour_tile: int32 [1024, 8], replicated, may hold values from 0 to 15
- seam_rotation: int32 [1024, 8], replicated, may hold values from 0 to 3
Outputs:
- features: bfloat16 [2, 1024, 4, 4, 128], P('dp', 'tile')
- input_grad: float32 [2, 1024, 8, 8, 128], P('dp', 'tile')
- grad_first: float32 [1152, 128], P('dp')
- grad_second: float32 [1152, 128], P('dp')
- grad_down: float32 [512, 128], P('dp')
The draws below stay inside these ranges and needn't reach their ends.
Inputs may be any that keep to these rules, and one draw needn't show every extreme that they name: `edge_owner`: the four devices of a row differ. Among the rows of the 16 tiles of one device no device is named more than 2 times, and some device exactly 2 times. `corner_owner`: as for edge_owner.
All inputs are finite; a program needn't handle non-finite values.
Results may differ from the reference program's by a relative error of at most 0.0085.
Values may be sent and summed in bfloat16 or wider, within the bound.
A program may use at most 64 MiB of HBM per device.

```python
import math
import jax
import jax.numpy as jnp
import numpy as np
from jax import lax

C = 128
S = 8
TILE_DEV = 16
TILES = 1024
SAMPLES = 2
CAP = 2
N_TILE = 64


def set_ends(array, own_key, low, top_value):
    index_at = [jax.random.randint(jax.random.fold_in(own_key, axis), (), 0, length) for axis, length in enumerate(array.shape)]
    main_axis = array.shape.index(max(array.shape))
    beside = index_at[:main_axis] + [(index_at[main_axis] + 1) % array.shape[main_axis]] + index_at[main_axis + 1:]
    return array.at[tuple(index_at)].set(low).at[tuple(beside)].set(top_value)


def block_scale(key, shape, cuts, low, largest):
    def one(axis_at, blocks):
        draws = jax.random.uniform(jax.random.fold_in(jax.random.fold_in(key, 6), axis_at), (blocks,), jnp.float32, low / len(cuts), largest / len(cuts))
        return jnp.repeat(jnp.exp(draws), shape[axis_at] // blocks).reshape((-1,) + (1,) * (len(shape) - axis_at - 1))

    loudness = one(*cuts[0])
    for cut in cuts[1:]:
        loudness = loudness * one(*cut)
    return loudness


def deal_out(key, own, number, rows, number_of, top, reach, skew):
    sequence = jax.random.permutation(key, number_of)
    crowded, common = load_shares(number_of, rows * top, reach, skew, True), load_shares(number_of, rows * top, reach, skew, False)
    places = jnp.arange(number_of)

    def named(lengths, offset_by):
        used = int((lengths > 0).sum())
        fixed = max(1, used // 4)
        moved = fixed + (places - fixed + offset_by * (used - fixed)) % max(1, number_of - fixed)
        return jnp.zeros((number_of,), jnp.int32).at[sequence[jnp.where(places < fixed, places, moved)]].set(jnp.asarray(lengths, jnp.int32))

    lengths = jnp.where(number % 4 == 0, named(crowded, number // 4), named(common, number - number // 4 - 1))
    mixed = jax.random.permutation(jax.random.fold_in(own, 3), number_of)
    giver, sink = mixed[0:number_of // 2 * 2:2], mixed[1:number_of // 2 * 2:2]
    room = jnp.minimum(lengths[giver] - 1, reach - lengths[sink]) // 2
    room = jnp.where((giver == sequence[0]) | (sink == sequence[0]) | (lengths[sink] == 0), 0, jnp.maximum(room, 0))
    moved = jax.random.randint(jax.random.fold_in(own, 4), (number_of // 2,), 0, 1 << 20) % (room + 1)
    lengths = lengths.at[giver].add(-moved).at[sink].add(moved)
    items = jnp.searchsorted(jnp.cumsum(lengths), jnp.arange(rows * top), side="right").astype(jnp.int32)
    grid = items.reshape(top, rows).T
    grid = grid[jax.random.permutation(jax.random.fold_in(own, 1), rows)]
    offset_by = jax.random.randint(jax.random.fold_in(own, 2), (rows, 1), 0, top)
    return jnp.take_along_axis(grid, (jnp.arange(top)[None, :] + offset_by) % top, axis=1)


def load_shares(number_of, total, reach, lean, full):
    portions = [(1 << 20) // math.isqrt(rank ** lean) + 1 for rank in range(1, number_of + 1)]
    largest = reach if full else min(reach, max(-(-total // number_of), total * portions[0] // sum(portions)))
    least = 1 if total - largest >= number_of - 1 else 0
    counts, rest = [largest] + [least] * (number_of - 1), total - largest - least * (number_of - 1)
    while rest > 0:
        free = [i for i in range(1, number_of) if counts[i] < largest] or [i for i in range(1, number_of) if counts[i] < reach]
        whole, remaining = sum([portions[i] for i in free]), rest
        for i in free:
            more = min(reach - counts[i], max(1, remaining * portions[i] // whole), rest)
            counts[i] = counts[i] + more
            rest = rest - more
    return np.array(counts)


def centred(own_key, shape, spread, most, shards=(), kind=jnp.bfloat16):
    values = spread * jax.random.normal(own_key, shape, jnp.float32)
    if shards:
        values = values * block_scale(own_key, shape, shards, -0.22, 0.18)
    return jnp.clip(values, -most, most).astype(kind)


def setup_inputs(seed: int = 0) -> dict:
    splits = jax.random.split(jax.random.key(seed), 10)
    inputs = centred(splits[0], (SAMPLES, TILES, S, S, C), 1.0, 6.0, ((0, 2), (1, 64)))
    cotangent = centred(splits[1], (SAMPLES, TILES, S // 2, S // 2, C), 1.0, 6.0, ((0, 2), (1, 64)))
    w_first = centred(splits[2], (9 * C, C), (9 * C) ** -0.5, 0.1875)
    w_second = centred(splits[3], (9 * C, C), (9 * C) ** -0.5, 0.1875)
    w_down = centred(splits[4], (4 * C, C), (4 * C) ** -0.5, 0.25)
    edge_owner_keys = jax.random.split(jax.random.fold_in(splits[5], 1), TILES // TILE_DEV)
    edge_owner_turns = jax.random.permutation(jax.random.fold_in(splits[5], 3), TILES // TILE_DEV)
    edge_owner = jax.vmap(lambda own, number: deal_out(jax.random.fold_in(splits[5], 2), own, number, TILE_DEV, N_TILE, 4, CAP, 2))(edge_owner_keys, edge_owner_turns).reshape((TILES, 4))
    corner_owner_keys = jax.random.split(jax.random.fold_in(splits[6], 1), TILES // TILE_DEV)
    corner_owner_turns = jax.random.permutation(jax.random.fold_in(splits[6], 3), TILES // TILE_DEV)
    corner_owner = jax.vmap(lambda own, number: deal_out(jax.random.fold_in(splits[6], 2), own, number, TILE_DEV, N_TILE, 4, CAP, 2))(corner_owner_keys, corner_owner_turns).reshape((TILES, 4))
    neighbour_tile = set_ends(jax.random.randint(splits[7], (TILES, 8), 0, TILE_DEV), jax.random.fold_in(splits[7], 1), 0, TILE_DEV - 1).astype(jnp.int32)
    seam_rotation = set_ends(jax.random.randint(splits[8], (TILES, 8), 0, 4), jax.random.fold_in(splits[8], 1), 0, 3).astype(jnp.int32)
    return dict(inputs=inputs, cotangent=cotangent, w_first=w_first, w_second=w_second, w_down=w_down, edge_owner=edge_owner, corner_owner=corner_owner, neighbour_tile=neighbour_tile, seam_rotation=seam_rotation)


def rotations(tile_data):
    return jnp.stack([jnp.rot90(tile_data, quarter, axes=(0, 1)) for quarter in range(4)])

def pad_field(field, neighbour_ids, seam_rotation):

    def build(packed):
        own_tile, id_row, turn_row = packed
        turned = [rotations(field[id_row[slot]])[turn_row[slot]] for slot in range(8)]
        north_rim = turned[0][-1:, :]
        east_rim = turned[1][:, :1]
        south_rim = turned[2][:1, :]
        west_rim = turned[3][:, -1:]
        top_row = jnp.concatenate([turned[7][-1:, -1:], north_rim, turned[4][-1:, :1]], axis=1)
        middle_band = jnp.concatenate([west_rim, own_tile, east_rim], axis=1)
        bottom_row = jnp.concatenate([turned[6][:1, -1:], south_rim, turned[5][:1, :1]], axis=1)
        return jnp.concatenate([top_row, middle_band, bottom_row], axis=0)
    return lax.map(build, (field, neighbour_ids, seam_rotation))

def pad_adjoint(back_pad, neighbour_ids, seam_rotation):
    zeros_field = jnp.zeros((TILES, S, S, C), jnp.float32)
    _, pull_back = jax.vjp(lambda values: pad_field(values, neighbour_ids, seam_rotation), zeros_field)
    return pull_back(back_pad)[0]

def conv_three(padded, weight):
    running = jnp.zeros((TILES * S * S, C), jnp.float32)
    for row_off in range(3):
        for col_off in range(3):
            tap_rows = padded[:, row_off:row_off + S, col_off:col_off + S].reshape(-1, C)
            tap_start = (3 * row_off + col_off) * C
            running = running + jnp.dot(tap_rows, weight[tap_start:tap_start + C], preferred_element_type=jnp.float32)
    return running.reshape(TILES, S, S, C)

def conv_weight_grad(padded, slope):
    slope_rows = slope.reshape(-1, C)
    pieces = []
    for row_off in range(3):
        for col_off in range(3):
            tap_rows = padded[:, row_off:row_off + S, col_off:col_off + S].reshape(-1, C)
            pieces.append(jnp.dot(tap_rows.T, slope_rows, preferred_element_type=jnp.float32))
    return jnp.concatenate(pieces, axis=0)

def conv_adjoint(slope, weight):
    slope_rows = slope.reshape(-1, C)
    back_pad = jnp.zeros((TILES, S + 2, S + 2, C), jnp.float32)
    for row_off in range(3):
        for col_off in range(3):
            tap_start = (3 * row_off + col_off) * C
            contrib = jnp.dot(slope_rows, weight[tap_start:tap_start + C].T, preferred_element_type=jnp.float32)
            back_pad = back_pad.at[:, row_off:row_off + S, col_off:col_off + S].add(contrib.reshape(TILES, S, S, C))
    return back_pad

def down_blocks(hidden):
    return hidden.reshape(TILES, S // 2, 2, S // 2, 2, C)

def down_forward(hidden, w_down):
    blocks = down_blocks(hidden)
    running = jnp.zeros((TILES * (S // 2) * (S // 2), C), jnp.float32)
    for row_off in range(2):
        for col_off in range(2):
            tap_rows = blocks[:, :, row_off, :, col_off].reshape(-1, C)
            tap_start = (2 * row_off + col_off) * C
            running = running + jnp.dot(tap_rows, w_down[tap_start:tap_start + C], preferred_element_type=jnp.float32)
    return running.reshape(TILES, S // 2, S // 2, C)

def down_adjoint(cot, w_down):
    cot_rows = cot.reshape(-1, C)
    outer_list = []
    for row_off in range(2):
        inner_list = []
        for col_off in range(2):
            tap_start = (2 * row_off + col_off) * C
            contrib = jnp.dot(cot_rows, w_down[tap_start:tap_start + C].T, preferred_element_type=jnp.float32)
            inner_list.append(contrib.reshape(TILES, S // 2, S // 2, C))
        outer_list.append(jnp.stack(inner_list, axis=3))
    return jnp.stack(outer_list, axis=2).reshape(TILES, S, S, C)

def down_weight_grad(hidden, cot):
    blocks = down_blocks(hidden)
    cot_rows = cot.reshape(-1, C)
    pieces = []
    for row_off in range(2):
        for col_off in range(2):
            tap_rows = blocks[:, :, row_off, :, col_off].reshape(-1, C)
            pieces.append(jnp.dot(tap_rows.T, cot_rows, preferred_element_type=jnp.float32))
    return jnp.concatenate(pieces, axis=0)

def silu_slope(values):
    logistic = jax.nn.sigmoid(values)
    return logistic * (1.0 + values * (1.0 - logistic))

def reference(inputs, cotangent, w_first, w_second, w_down, edge_owner, corner_owner, neighbour_tile, seam_rotation):
    neighbour_ids = jnp.concatenate([edge_owner * TILE_DEV + neighbour_tile[:, :4], corner_owner * TILE_DEV + neighbour_tile[:, 4:]], axis=1).astype(jnp.int32)
    grad_scale = float(SAMPLES * TILES * S * S) ** (-0.5)
    feature_list = []
    input_list = []
    grad_one = jnp.zeros((9 * C, C), jnp.float32)
    grad_two = jnp.zeros((9 * C, C), jnp.float32)
    grad_low = jnp.zeros((4 * C, C), jnp.float32)
    for sample in range(SAMPLES):
        pad_inputs = pad_field(inputs[sample], neighbour_ids, seam_rotation)
        pre_first = conv_three(pad_inputs, w_first)
        hidden_first = jax.nn.silu(pre_first).astype(jnp.bfloat16)
        pad_hidden = pad_field(hidden_first, neighbour_ids, seam_rotation)
        pre_second = conv_three(pad_hidden, w_second)
        hidden_second = jax.nn.silu(pre_second).astype(jnp.bfloat16)
        feature_list.append(down_forward(hidden_second, w_down).astype(jnp.bfloat16))
        cot = cotangent[sample]
        grad_low = grad_low + down_weight_grad(hidden_second, cot) * grad_scale
        back_second = down_adjoint(cot, w_down)
        slope_second = (back_second * silu_slope(pre_second)).astype(jnp.bfloat16)
        grad_two = grad_two + conv_weight_grad(pad_hidden, slope_second) * grad_scale
        back_first = pad_adjoint(conv_adjoint(slope_second, w_second), neighbour_ids, seam_rotation)
        slope_first = (back_first * silu_slope(pre_first)).astype(jnp.bfloat16)
        grad_one = grad_one + conv_weight_grad(pad_inputs, slope_first) * grad_scale
        input_list.append(pad_adjoint(conv_adjoint(slope_first, w_first), neighbour_ids, seam_rotation))
    return (jnp.stack(feature_list), jnp.stack(input_list), grad_one, grad_two, grad_low)
```

```python
import jax
import jax.numpy as jnp
import numpy as np
from jax import lax
from jax.experimental import pallas as pl
from jax.experimental.pallas import tpu as pltpu
from jax.sharding import PartitionSpec as P

MESH = pl.DeviceIdType.MESH
F32 = jnp.float32
BF16 = jnp.bfloat16
N_TILE = 64
T = 16
S = 8
C = 128
PIX = S * S * T
TAPS = [(p, q) for p in range(3) for q in range(3)]
GRAD_SCALE = float(2 * 1024 * 64) ** -0.5
NB_LATE = (36 + 16, 36)


def seam_lines():
    grid = np.arange(S * S).reshape(S, S)
    first = np.zeros((8, 4), int)
    step = np.zeros((8, 4), int)
    for turn in range(4):
        turned = np.rot90(grid, turn)
        lines = [turned[-1, :], turned[:, 0], turned[0, :], turned[:, -1]]
        for k, line in enumerate(lines):
            first[k, turn], step[k, turn] = line[0], line[1] - line[0]
        cells = [turned[-1, 0], turned[0, 0], turned[0, -1], turned[-1, -1]]
        for k, cell in enumerate(cells):
            first[4 + k, turn] = cell
    return first, step


def iota(shape, axis):
    return lax.broadcasted_iota(jnp.int32, shape, axis)


def hot(mask):
    return jnp.where(mask, 1.0, 0.0).astype(BF16)


def mm(a, b):
    return jnp.dot(a, b, preferred_element_type=F32)


def mm_nt(a, b):
    return lax.dot_general(a, b, (((1,), (1,)), ((), ())), preferred_element_type=F32)


def kernel(
    x_ref, cot_ref, w1_ref, w2_ref, wd_ref, eo_ref, co_ref, nb_ref, rot_ref,
    feat_ref, ig_ref, o1_ref, o2_ref, od_ref,
    wide, bp, pre1, pad1, pad2, slope_pad, g_mat, gt_mat, gc_mat, gct_mat,
    r_mat, rt_mat, rc_mat, rct_mat, w1t, w2t, wdt, back2, hid2, cot_p, cot_t, slope_t,
    small, gf0, gf1, s_a0, s_a1, r_a0, r_a1, s_b, r_b, s_c, r_c0, r_c1,
    s_edge, r_edge, s_corner, r_corner,
    ex_send, ex_recv, red_send, red_recv,
):
    dp = lax.axis_index("dp")
    me = lax.axis_index("tile")
    core = lax.rem(me, 2)
    chip = dp * 32 + lax.div(me, 2)
    flat = dp * N_TILE + me
    barrier = pltpu.get_barrier_semaphore()

    def greet(o, carry):
        other = lax.rem(flat + o, 2 * N_TILE)
        pl.semaphore_signal(
            barrier, inc=1,
            device_id=(lax.div(other, N_TILE), lax.rem(other, N_TILE)), device_id_type=MESH,
        )
        return carry

    lax.fori_loop(1, 2 * N_TILE, greet, 0)

    me_f = me.astype(F32)
    own = jnp.concatenate([eo_ref[...], co_ref[...]], axis=0).astype(F32)
    src = nb_ref[...].astype(F32)
    rot = rot_ref[...].astype(F32)
    row8 = iota((8, 1024), 0)
    first, step = seam_lines()
    base_v = jnp.zeros((8, 1024), F32)
    step_v = jnp.zeros((8, 1024), F32)
    for turn in range(4):
        bcol = jnp.zeros((8, 1024), F32)
        scol = jnp.zeros((8, 1024), F32)
        for k in range(8):
            bcol = jnp.where(row8 == k, float(first[k, turn]), bcol)
            scol = jnp.where(row8 == k, float(step[k, turn]), scol)
        base_v = jnp.where(rot == float(turn), bcol, base_v)
        step_v = jnp.where(rot == float(turn), scol, step_v)
    match = jnp.where(own == me_f, 1.0, 0.0)

    def per_kind(v):
        a = jnp.broadcast_to(jnp.sum(v[0:4], axis=0, keepdims=True), (4, 1024))
        b = jnp.broadcast_to(jnp.sum(v[4:8], axis=0, keepdims=True), (4, 1024))
        return jnp.concatenate([a, b], axis=0)

    has = per_kind(match)
    lane16 = jnp.bitwise_and(iota((8, 1024), 1), 15)
    acc = has
    for sh in (1, 2, 4, 8):
        acc = acc + jnp.where(lane16 >= sh, pltpu.roll(acc, sh, 1), 0.0)
    rank = acc - has
    table = []
    for s in range(2):
        sel = match * jnp.where(rank == float(s), 1.0, 0.0)
        for v in (sel, sel * base_v, sel * step_v, sel * src):
            table.append(per_kind(v))
    tab = jnp.concatenate([v[0:1] for v in table] + [v[4:5] for v in table], axis=0).astype(BF16)
    lane_i = iota((1, 1024), 1)
    sub_i = iota((1024, 1), 0)
    lane_f = lane_i.astype(F32)
    sub_f = sub_i.astype(F32)
    blk_l = jnp.right_shift(lane_i, 4).astype(F32)
    blk_s = jnp.right_shift(sub_i, 4).astype(F32)
    block_diag = hot(blk_s == blk_l)
    slots_e = mm(tab, block_diag)
    pair_s = jnp.right_shift(iota((128, 1), 0), 1).astype(F32)
    slots_c = mm_nt(tab, hot(pair_s == blk_l))

    def target(rows, which, px):
        v0, b0, t0, n0, v1, b1, t1, n1 = [rows[i:i + 1] for i in range(8)]
        late = which > 0.5
        valid = jnp.where(late, v1, v0)
        pixel = jnp.where(late, b1, b0) + jnp.where(late, t1, t0) * px
        return jnp.where(valid > 0.5, pixel * float(T) + jnp.where(late, n1, n0), -1.0)

    te = target(
        slots_e[0:8],
        jnp.bitwise_and(jnp.right_shift(lane_i, 3), 1).astype(F32),
        jnp.bitwise_and(lane_i, 7).astype(F32),
    )
    tc = target(slots_c[8:16], jnp.bitwise_and(lane_i[:, :128], 1).astype(F32), 0.0)

    def as_column(row, n):
        return jnp.transpose(jnp.broadcast_to(row, (128, n)))[:, 0:1]

    g_mat[...] = hot(as_column(te, 1024) == lane_f)
    gc_mat[...] = hot(as_column(tc, 128) == lane_f)

    pad1[...] = jnp.zeros_like(pad1)
    wide[...] = x_ref[...].astype(F32)
    for px in range(S * S):
        pad1[1 + px // S, 1 + px % S] = wide[pl.ds(px, T, stride=S * S), :].astype(BF16)

    def pack(n, edges, corners):
        s_edge[n] = edges.astype(BF16).reshape(N_TILE, T, C)
        s_corner[n] = corners.astype(BF16).reshape(N_TILE, 2, C)

    def gather(n, field):
        pack(n, mm(g_mat[...], field), mm(gc_mat[...], field))

    def exchange(n, d):
        e = pltpu.make_async_remote_copy(
            src_ref=s_edge.at[n, d], dst_ref=r_edge.at[n, me],
            send_sem=ex_send.at[n, 0], recv_sem=ex_recv.at[n, 0],
            device_id=(dp, d), device_id_type=MESH,
        )
        c = pltpu.make_async_remote_copy(
            src_ref=s_corner.at[n, d], dst_ref=r_corner.at[n, me],
            send_sem=ex_send.at[n, 1], recv_sem=ex_recv.at[n, 1],
            device_id=(dp, d), device_id_type=MESH,
        )
        return e, c

    def ex_start(n):
        def send(o, carry):
            e, c = exchange(n, lax.rem(me + o, N_TILE))
            e.start()
            c.start()
            return carry

        lax.fori_loop(1, N_TILE, send, 0)
        r_edge[n, me] = s_edge[n, me]
        r_corner[n, me] = s_corner[n, me]

    def ex_all(n):
        rest = pl.ds(0, N_TILE - 1)
        to = (dp, lax.rem(me + 1, N_TILE))
        e = pltpu.make_async_remote_copy(
            src_ref=s_edge.at[n, rest], dst_ref=r_edge.at[n, rest],
            send_sem=ex_send.at[n, 0], recv_sem=ex_recv.at[n, 0],
            device_id=to, device_id_type=MESH,
        )
        c = pltpu.make_async_remote_copy(
            src_ref=s_corner.at[n, rest], dst_ref=r_corner.at[n, rest],
            send_sem=ex_send.at[n, 1], recv_sem=ex_recv.at[n, 1],
            device_id=to, device_id_type=MESH,
        )
        return e, c

    def ex_wait(n):
        e, c = ex_all(n)
        e.wait_recv()
        c.wait_recv()
        return r_edge[n].reshape(N_TILE * T, C), r_corner[n].reshape(2 * N_TILE, C)

    gather(0, pad1[1:9, 1:9].reshape(PIX, C))
    pl.semaphore_wait(barrier, 2 * N_TILE - 1)
    ex_start(0)

    ownb = own.astype(BF16)
    pick = hot(iota((128, 1), 0).astype(F32) + me_f * float(T) == lane_f)
    my_row = mm_nt(ownb, pick)
    my_col = mm_nt(pick[0:16], ownb)
    earlier = iota((T, 128), 1).astype(F32) < iota((T, 128), 0).astype(F32)

    def slot_base(kind, per_owner, per_rank):
        out = []
        for k in range(4 * kind, 4 * kind + 4):
            col = my_col[:, k:k + 1]
            shared = jnp.zeros((T, 128), F32)
            for k2 in range(4 * kind, 4 * kind + 4):
                shared = shared + jnp.where(col == my_row[k2:k2 + 1], 1.0, 0.0)
            rk = jnp.sum(jnp.where(earlier, shared, 0.0), axis=1, keepdims=True)
            out.append(col * per_owner + rk * per_rank)
        return out

    base_e = slot_base(0, 16.0, 8.0)
    base_c = slot_base(1, 2.0, 1.0)
    col_e = jnp.concatenate([b + float(px) for b in base_e for px in range(S)], axis=0)
    col_c = jnp.concatenate(base_c + [jnp.full((64, 1), -1.0, F32)], axis=0)
    r_mat[...] = hot(col_e == lane_f)
    rc_mat[...] = hot(col_c == lane_f[:, :128])
    row_e = jnp.transpose(jnp.broadcast_to(col_e, (512, 128)))[0:1]
    row_c = jnp.transpose(jnp.broadcast_to(col_c, (128, 128)))[0:1]
    rt_mat[...] = hot(sub_f == row_e)
    rct_mat[...] = hot(sub_f[:128] == row_c)
    gt_mat[...] = hot(sub_f == te)
    gct_mat[...] = hot(sub_f == tc)

    def flip(w):
        return jnp.transpose(w.astype(F32)).astype(BF16)

    for tap in range(9):
        at = slice(tap * C, tap * C + C)
        w1t[at] = flip(w1_ref[at])
        w2t[at] = flip(w2_ref[at])
    for tap in range(4):
        at = slice(tap * C, tap * C + C)
        wdt[at] = flip(wd_ref[at])
    small[...] = cot_ref[...].astype(F32)
    for px in range(16):
        cot_p[pl.ds(px * T, T), :] = small[pl.ds(px, T, stride=16), :].astype(BF16)
    cot_t[...] = flip(cot_p[...])
    for tap in range(4):
        back = mm(cot_p[...], wdt[tap * C:tap * C + C]).reshape(4, 4, T, C)
        back2[:, tap // 2, :, tap % 2] = back
    pad2[...] = jnp.zeros_like(pad2)
    slope_pad[...] = jnp.zeros_like(slope_pad)

    def fill_rims(n, pad):
        edges, corners = ex_wait(n)
        rims = mm(r_mat[...], edges).astype(BF16).reshape(4, S, T, C)
        cells = mm(rc_mat[...], corners).astype(BF16)
        pad[0, 1:9] = rims[0]
        pad[1:9, 9] = rims[1]
        pad[9, 1:9] = rims[2]
        pad[1:9, 0] = rims[3]
        pad[0, 9] = cells[0:16]
        pad[9, 9] = cells[16:32]
        pad[9, 0] = cells[32:48]
        pad[0, 0] = cells[48:64]

    def taps_sum(read, w):
        out = None
        for a in range(0, 9, 2):
            taps = TAPS[a:a + 2]
            lhs = [read(p, q) for p, q in taps]
            lhs = lhs[0] if len(lhs) == 1 else jnp.concatenate(lhs, axis=1)
            part = mm(lhs, w[a * C:(a + len(taps)) * C])
            out = part if out is None else out + part
        return out

    def conv(pad, w, i):
        return taps_sum(lambda p, q: pad[i + p:i + p + 2, q:q + 8].reshape(256, C), w)

    def logistic(v):
        return 1.0 / (1.0 + jnp.exp(-v))

    fill_rims(0, pad1)
    for i in range(0, S, 2):
        v = conv(pad1, w1_ref, i)
        pre1[i:i + 2] = v.reshape(2, S, T, C)
        pad2[1 + i:3 + i, 1:9] = (v * logistic(v)).astype(BF16).reshape(2, S, T, C)
    gather(1, pad2[1:9, 1:9].reshape(PIX, C))
    ex_start(1)
    fill_rims(1, pad2)
    for i in range(0, S, 2):
        v = conv(pad2, w2_ref, i)
        s = logistic(v)
        hid2[i // 2] = (v * s).astype(BF16).reshape(2, 4, 2, T, C)
        d = back2[i // 2].reshape(256, C) * (s * (1.0 + v * (1.0 - s)))
        slope_pad[2 + i:4 + i, 2:10] = d.astype(BF16).reshape(2, S, T, C)
        slope_t[:, i * 128:i * 128 + 256] = jnp.transpose(d).astype(BF16)

    def conv_back(wt):
        for a in range(0, 10, 2):
            v = taps_sum(
                lambda p, q: slope_pad[a + 2 - p:a + 4 - p, 2 - q:12 - q].reshape(320, C), wt
            )
            bp[a:a + 2] = v.reshape(2, 10, T, C)

    def return_rims(n):
        rims = [bp[0, 1:9], bp[1:9, 9], bp[9, 1:9], bp[1:9, 0]]
        edges = jnp.concatenate([r.astype(BF16).reshape(S * T, C) for r in rims], axis=0)
        cells = [bp[0, 9], bp[9, 9], bp[9, 0], bp[0, 0], jnp.zeros((64, C), F32)]
        corners = jnp.concatenate(cells, axis=0).astype(BF16)
        pack(n, mm(rt_mat[...], edges), mm(rct_mat[...], corners))
        ex_start(n)

    def returned(n):
        edges, corners = ex_wait(n)
        inner = bp[1:9, 1:9].reshape(PIX, C)
        return inner + mm(gt_mat[...], edges) + mm(gct_mat[...], corners)

    conv_back(w2t)
    return_rims(2)

    def hid_tap(p, q):
        return hid2[:, p, :, q].reshape(256, C)

    feats = None
    for tap in range(4):
        part = mm(hid_tap(tap // 2, tap % 2), wd_ref[tap * C:tap * C + C])
        feats = part if feats is None else feats + part
    small[...] = feats
    for t in range(T):
        feat_ref[pl.ds(t * 16, 16), :] = small[pl.ds(t, 16, stride=T), :].astype(BF16)

    def put(gf, tap, per_half, at, value):
        value = jnp.transpose(value).reshape(8, 16, C)
        low = tap * 8
        for half in range(2):
            lo, hi = max(low, half * per_half), min(low + 8, (half + 1) * per_half)
            if lo < hi:
                gf[half, at + lo - half * per_half:at + hi - half * per_half] = (
                    value[lo - low:hi - low]
                )

    for tap in range(4):
        put(gf0, tap, 16, 36, mm(cot_t[...], hid_tap(tap // 2, tap % 2)))

    def weight_grad(pad, gf):
        for a in range(0, 9, 2):
            taps = TAPS[a:a + 2]
            rhs = [pad[p:p + 8, q:q + 8].reshape(PIX, C) for p, q in taps]
            rhs = rhs[0] if len(rhs) == 1 else jnp.concatenate(rhs, axis=1)
            both = mm(slope_t[...], rhs)
            for j in range(len(taps)):
                put(gf, a + j, 36, 0, both[:, j * C:(j + 1) * C])

    weight_grad(pad2, gf0)

    late = ((gf0, s_a0, r_a0, r_c0), (gf1, s_a1, r_a1, r_c1))

    def swap(n):
        gf, s_a, r_a, _ = late[n]
        return pltpu.make_async_remote_copy(
            src_ref=s_a, dst_ref=r_a, send_sem=red_send.at[n, 0], recv_sem=red_recv.at[n, 0],
            device_id=(dp, me + 1 - 2 * core), device_id_type=MESH,
        )

    def swap_start(n):
        gf, s_a, r_a, _ = late[n]
        s_a[...] = (gf[1 - core] * GRAD_SCALE).astype(BF16)
        swap(n).start()

    def block_copy(n, b):
        return pltpu.make_async_remote_copy(
            src_ref=s_b.at[n, b], dst_ref=r_b.at[n, chip],
            send_sem=red_send.at[n, 1], recv_sem=red_recv.at[n, 1],
            device_id=(lax.div(b, 32), lax.rem(b, 32) * 2 + core), device_id_type=MESH,
        )

    def block_many(n, count):
        at = pl.ds(0, count)
        return pltpu.make_async_remote_copy(
            src_ref=s_b.at[n, at], dst_ref=r_b.at[n, at],
            send_sem=red_send.at[n, 1], recv_sem=red_recv.at[n, 1],
            device_id=(dp, me + 1 - 2 * core), device_id_type=MESH,
        )

    def scatter_start(n):
        gf, s_a, r_a, _ = late[n]
        nb = NB_LATE[n]
        swap(n).wait_recv()
        s_b[n, 0:nb] = (gf[core] * GRAD_SCALE + r_a[...].astype(F32)).astype(BF16)

        def send(o, carry):
            b = lax.rem(chip + o, 64)

            @pl.when(b < nb)
            def _():
                block_copy(n, b).start()

            return carry

        lax.fori_loop(1, 64, send, 0)

        @pl.when(chip < nb)
        def _():
            r_b[n, chip] = s_b[n, chip]

    def share_copy(n, t):
        return pltpu.make_async_remote_copy(
            src_ref=s_c.at[n], dst_ref=late[n][3].at[chip],
            send_sem=red_send.at[n, 2], recv_sem=red_recv.at[n, 2],
            device_id=(core, t), device_id_type=MESH,
        )

    def share_many(n, count):
        at = pl.ds(0, count)
        return pltpu.make_async_remote_copy(
            src_ref=r_b.at[n, at], dst_ref=r_b.at[n, at],
            send_sem=red_send.at[n, 2], recv_sem=red_recv.at[n, 2],
            device_id=(dp, me + 1 - 2 * core), device_id_type=MESH,
        )

    def share_start(n):
        nb = NB_LATE[n]

        @pl.when(chip < nb)
        def _():
            block_many(n, 63).wait_recv()
            total = jnp.sum(r_b[n].astype(F32), axis=0)
            s_c[n] = total.astype(BF16)

            def send(o, carry):
                share_copy(n, lax.rem(me + o, N_TILE)).start()
                return carry

            lax.fori_loop(1, N_TILE, send, 0)

            @pl.when(dp != core)
            def _():
                share_copy(n, me).start()

            @pl.when(dp == core)
            def _():
                late[n][3][chip] = s_c[n]

    def share_wait(n):
        nb = NB_LATE[n]
        mine = jnp.logical_and(chip < nb, dp == core)

        @pl.when(mine)
        def _():
            share_many(n, nb - 1).wait_recv()

        @pl.when(jnp.logical_not(mine))
        def _():
            share_many(n, nb).wait_recv()

    swap_start(0)

    scatter_start(0)
    grad = returned(2)
    for i in range(0, S, 2):
        v = pre1[i:i + 2].reshape(256, C)
        s = logistic(v)
        d = grad[i * 128:i * 128 + 256] * (s * (1.0 + v * (1.0 - s)))
        slope_pad[2 + i:4 + i, 2:10] = d.astype(BF16).reshape(2, S, T, C)
        slope_t[:, i * 128:i * 128 + 256] = jnp.transpose(d).astype(BF16)
    weight_grad(pad1, gf1)
    swap_start(1)
    conv_back(w1t)
    return_rims(3)
    scatter_start(1)
    share_start(0)
    wide[...] = returned(3)
    for t in range(T):
        ig_ref[pl.ds(t * 64, 64), :] = wide[pl.ds(t, 64, stride=T), :]
    share_start(1)
    share_wait(0)
    o2_ref[...] = r_c0[0:36].astype(F32).reshape(576, C)
    od_ref[...] = r_c0[36:52].astype(F32).reshape(256, C)
    share_wait(1)
    o1_ref[...] = r_c1[...].astype(F32).reshape(576, C)

    for n in range(4):
        e, c = ex_all(n)
        e.wait_send()
        c.wait_send()
    for n in range(2):
        nb = NB_LATE[n]
        swap(n).wait_send()

        @pl.when(chip < nb)
        def _():
            block_many(n, nb - 1).wait_send()

            @pl.when(dp == core)
            def _():
                share_many(n, 63).wait_send()

            @pl.when(dp != core)
            def _():
                share_many(n, 64).wait_send()

        @pl.when(chip >= nb)
        def _():
            block_many(n, nb).wait_send()


def local(inputs, cotangent, w_first, w_second, w_down, edge_owner, corner_owner, neighbour_tile, seam_rotation):
    vmem = pl.BlockSpec(memory_space=pltpu.VMEM)
    v = pltpu.VMEM
    outs = pl.pallas_call(
        kernel,
        out_shape=(
            jax.ShapeDtypeStruct((256, C), BF16),
            jax.ShapeDtypeStruct((1024, C), F32),
            jax.ShapeDtypeStruct((576, C), F32),
            jax.ShapeDtypeStruct((576, C), F32),
            jax.ShapeDtypeStruct((256, C), F32),
        ),
        in_specs=[vmem] * 9,
        out_specs=(vmem,) * 5,
        scratch_shapes=[
            v((1024, C), F32),
            v((10, 10, T, C), F32),
            v((S, S, T, C), F32),
            v((10, 10, T, C), BF16),
            v((10, 10, T, C), BF16),
            v((12, 12, T, C), BF16),
            v((1024, 1024), BF16),
            v((1024, 1024), BF16),
            v((128, 1024), BF16),
            v((1024, 128), BF16),
            v((512, 1024), BF16),
            v((1024, 512), BF16),
            v((128, 128), BF16),
            v((128, 128), BF16),
            v((1152, C), BF16),
            v((1152, C), BF16),
            v((512, C), BF16),
            v((4, 2, 4, 2, T, C), F32),
            v((4, 2, 4, 2, T, C), BF16),
            v((256, C), BF16),
            v((C, 256), BF16),
            v((C, 1024), BF16),
            v((256, C), F32),
            v((2, 52, 16, C), F32),
            v((2, 36, 16, C), F32),
            v((52, 16, C), BF16),
            v((36, 16, C), BF16),
            v((52, 16, C), BF16),
            v((36, 16, C), BF16),
            v((2, 64, 16, C), BF16),
            v((2, 64, 16, C), BF16),
            v((2, 16, C), BF16),
            v((52, 16, C), BF16),
            v((36, 16, C), BF16),
            v((4, N_TILE, T, C), BF16),
            v((4, N_TILE, T, C), BF16),
            v((4, N_TILE, 2, C), BF16),
            v((4, N_TILE, 2, C), BF16),
            pltpu.SemaphoreType.DMA((4, 2)),
            pltpu.SemaphoreType.DMA((4, 2)),
            pltpu.SemaphoreType.DMA((2, 3)),
            pltpu.SemaphoreType.DMA((2, 3)),
        ],
        compiler_params=pltpu.CompilerParams(
            collective_id=0, has_side_effects=True, vmem_limit_bytes=60 * 1024 * 1024
        ),
    )(
        inputs.reshape(1024, C), cotangent.reshape(256, C), w_first, w_second, w_down,
        edge_owner.T, corner_owner.T, neighbour_tile.T, seam_rotation.T,
    )
    feats, grads, one, two, low = outs
    return (feats.reshape(1, T, 4, 4, C), grads.reshape(1, T, S, S, C), one, two, low)


def solution(mesh):
    tiles = P("dp", "tile", None, None, None)
    return jax.shard_map(
        local,
        mesh=mesh,
        in_specs=(tiles, tiles) + (P(),) * 7,
        out_specs=(tiles, tiles) + (P("dp", None),) * 3,
        check_vma=False,
    )
```

```python
import itertools

import jax
import jax.numpy as jnp
import numpy as np
from jax import lax
from jax.experimental import pallas as pl
from jax.experimental.pallas import tpu as pltpu
from jax.sharding import PartitionSpec as P

MESH = pl.DeviceIdType.MESH
F32 = jnp.float32
BF16 = jnp.bfloat16
N_TILE = 64
T = 16
S = 8
C = 128
PIX = S * S * T
TAPS = [(p, q) for p in range(3) for q in range(3)]
GRAD_SCALE = float(2 * 1024 * 64) ** -0.5
BLOCKS = (36 + 16, 36)


def hops(rel):
    return min(rel[0], 4 - rel[0]) + rel[1] + min(rel[2], 4 - rel[2]) + 0.3 * rel[3]


OFFSETS = sorted(itertools.product(range(4), range(2), range(4), range(2)), key=hops, reverse=True)
PEERS = OFFSETS[:-1]
EDGE_LINES = [(0, slice(0, 8)), (7, slice(0, 8)), (slice(1, 7), 0), (slice(1, 7), 7)]
INSIDE = (slice(1, 7), slice(1, 7))


def seam_lines():
    grid = np.arange(S * S).reshape(S, S)
    sides = [grid[0], grid[-1], grid[:, 0], grid[:, -1]]
    first = np.zeros((8, 4), int)
    step = np.zeros((8, 4), int)
    for turn in range(4):
        turned = np.rot90(grid, turn)
        lines = [turned[-1, :], turned[:, 0], turned[0, :], turned[:, -1]]
        for k, line in enumerate(lines):
            for n, side in enumerate(sides):
                if (line == side).all():
                    first[k, turn], step[k, turn] = 8 * n, 1
                if (line[::-1] == side).all():
                    first[k, turn], step[k, turn] = 8 * n + 7, -1
        cells = [turned[-1, 0], turned[0, 0], turned[0, -1], turned[-1, -1]]
        for k, cell in enumerate(cells):
            first[4 + k, turn] = {0: 0, 7: 7, 56: 8, 63: 15}[int(cell)]
    return first, step


def iota(shape, axis):
    return lax.broadcasted_iota(jnp.int32, shape, axis)


def hot(mask):
    return jnp.where(mask, 1.0, 0.0).astype(BF16)


def mm(a, b):
    return jnp.dot(a, b, preferred_element_type=F32)


def mm_nt(a, b):
    return lax.dot_general(a, b, (((1,), (1,)), ((), ())), preferred_element_type=F32)


def logistic(v):
    return 1.0 / (1.0 + jnp.exp(-v))


def silu_slope(v):
    s = logistic(v)
    return s * (1.0 + v * (1.0 - s))


def flip(w):
    return jnp.transpose(w.astype(F32)).astype(BF16)


def flat(v):
    return v.reshape(-1, C)


def cells(v):
    return v.reshape(-1, T, C)


def moved(region, by):
    return tuple(slice(r.start + by, r.stop + by) if isinstance(r, slice) else r + by for r in region)


def kernel(
    x_hbm, cot_hbm, w1_hbm, w2_hbm, wd_hbm, eo_hbm, co_hbm, nb_hbm, rot_hbm,
    feat_ref, ig_ref, late0_ref, late1_ref,
    x_ref, cot_ref, w1_ref, w2_ref, wd_ref, eo_ref, co_ref, nb_ref, rot_ref,
    wide, inner, pre1, pre2, pad1, pad2, slope_pad, g_mat, gt_mat, gc_mat, gct_mat,
    r_mat, rt_mat, rc_mat, rct_mat, w1t, w2t, wdt, back6, back2, hid2, cot_p, cot_t,
    small, gf0, gf1, s_a0, s_a1, r_a0, r_a1, s_b, r_b, s_c, r_c0, r_c1,
    s_edge, r_edge, s_corner, r_corner,
    load_sem, ex_send, ex_recv, red_send, red_recv,
):
    dp = lax.axis_index("dp")
    me = lax.axis_index("tile")
    core = lax.rem(me, 2)
    chip = dp * 32 + lax.div(me, 2)
    at_x = [lax.rem(lax.div(me, 16) + d, 4) * 16 for d in range(4)]
    at_z = [lax.rem(lax.div(me, 8) + d, 2) * 8 for d in range(2)]
    at_y = [lax.rem(lax.div(me, 2) + d, 4) * 2 for d in range(4)]
    at_c = [lax.rem(me + d, 2) for d in range(2)]

    def peer(rel):
        return at_x[rel[0]] + at_z[rel[1]] + at_y[rel[2]] + at_c[rel[3]]

    pairs = [
        (eo_hbm, eo_ref), (co_hbm, co_ref), (nb_hbm, nb_ref), (rot_hbm, rot_ref), (x_hbm, x_ref),
        (cot_hbm, cot_ref), (w1_hbm, w1_ref), (w2_hbm, w2_ref), (wd_hbm, wd_ref),
    ]
    loads = [pltpu.make_async_copy(a, b, load_sem.at[i]) for i, (a, b) in enumerate(pairs)]
    for load in loads:
        load.start()
    barrier = pltpu.get_barrier_semaphore()
    pl.semaphore_signal(barrier, inc=1, device_id=(1 - dp, me), device_id_type=MESH)
    for rel in PEERS:
        pl.semaphore_signal(barrier, inc=1, device_id=(dp, peer(rel)), device_id_type=MESH)
    for load in loads[:4]:
        load.wait()

    me_f = me.astype(F32)
    own = jnp.concatenate([eo_ref[...], co_ref[...]], axis=0).astype(F32)
    src = nb_ref[...].astype(F32)
    rot = rot_ref[...].astype(F32)
    row8 = iota((8, 1024), 0)
    first, step = seam_lines()
    base_v = jnp.zeros((8, 1024), F32)
    step_v = jnp.zeros((8, 1024), F32)
    for turn in range(4):
        bcol = jnp.zeros((8, 1024), F32)
        scol = jnp.zeros((8, 1024), F32)
        for k in range(8):
            bcol = jnp.where(row8 == k, float(first[k, turn]), bcol)
            scol = jnp.where(row8 == k, float(step[k, turn]), scol)
        base_v = jnp.where(rot == float(turn), bcol, base_v)
        step_v = jnp.where(rot == float(turn), scol, step_v)
    match = jnp.where(own == me_f, 1.0, 0.0)

    def per_kind(v):
        a = jnp.broadcast_to(jnp.sum(v[0:4], axis=0, keepdims=True), (4, 1024))
        b = jnp.broadcast_to(jnp.sum(v[4:8], axis=0, keepdims=True), (4, 1024))
        return jnp.concatenate([a, b], axis=0)

    has = per_kind(match)
    lane16 = jnp.bitwise_and(iota((8, 1024), 1), 15)
    acc = has
    for sh in (1, 2, 4, 8):
        acc = acc + jnp.where(lane16 >= sh, pltpu.roll(acc, sh, 1), 0.0)
    rank = acc - has
    table = []
    for s in range(2):
        sel = match * jnp.where(rank == float(s), 1.0, 0.0)
        for v in (sel, sel * base_v, sel * step_v, sel * src):
            table.append(per_kind(v))
    tab = jnp.concatenate([v[0:1] for v in table] + [v[4:5] for v in table], axis=0).astype(BF16)
    lane_i = iota((1, 1024), 1)
    sub_i = iota((1024, 1), 0)
    lane_f = lane_i.astype(F32)
    sub_f = sub_i.astype(F32)
    blk_l = jnp.right_shift(lane_i, 4).astype(F32)
    blk_s = jnp.right_shift(sub_i, 4).astype(F32)
    block_diag = hot(blk_s == blk_l)
    slots_e = mm(tab, block_diag)
    pair_s = jnp.right_shift(iota((128, 1), 0), 1).astype(F32)
    slots_c = mm_nt(tab, hot(pair_s == blk_l))

    def target(rows, which, px):
        v0, b0, t0, n0, v1, b1, t1, n1 = [rows[i:i + 1] for i in range(8)]
        late = which > 0.5
        valid = jnp.where(late, v1, v0)
        line = jnp.where(late, b1, b0) + jnp.where(late, t1, t0) * px
        return jnp.where(valid > 0.5, line * float(T) + jnp.where(late, n1, n0), -1.0)

    te = target(
        slots_e[0:8],
        jnp.bitwise_and(jnp.right_shift(lane_i, 3), 1).astype(F32),
        jnp.bitwise_and(lane_i, 7).astype(F32),
    )
    tc = target(slots_c[8:16], jnp.bitwise_and(lane_i[:, :128], 1).astype(F32), 0.0)

    def as_column(row, n):
        return jnp.transpose(jnp.broadcast_to(row, (128, n)))[:, 0:1]

    g_mat[...] = hot(as_column(te, 1024) == lane_f[:, :512])
    gc_mat[...] = hot(as_column(tc, 128) == lane_f[:, :512])

    pad1[...] = jnp.zeros_like(pad1)
    loads[4].wait()
    wide[...] = x_ref[...].astype(F32)
    for px in range(S * S):
        pad1[1 + px // S, 1 + px % S] = wide[pl.ds(px, T, stride=S * S), :].astype(BF16)

    def pack(n, edges, corners):
        s_edge[n] = edges.astype(BF16).reshape(N_TILE, T, C)
        s_corner[n] = corners.astype(BF16).reshape(N_TILE, 2, C)

    def gather(n, pad):
        lines = [pad[1, 1:9], pad[8, 1:9], pad[1:9, 1], pad[1:9, 8]]
        lines = jnp.concatenate([flat(v) for v in lines], axis=0)
        pack(n, mm(g_mat[...], lines), mm(gc_mat[...], lines))

    def ex_copies(n, src_at, dst_at, d):
        e = pltpu.make_async_remote_copy(
            src_ref=s_edge.at[n, src_at], dst_ref=r_edge.at[n, dst_at],
            send_sem=ex_send.at[n, 0], recv_sem=ex_recv.at[n, 0],
            device_id=(dp, d), device_id_type=MESH,
        )
        c = pltpu.make_async_remote_copy(
            src_ref=s_corner.at[n, src_at], dst_ref=r_corner.at[n, dst_at],
            send_sem=ex_send.at[n, 1], recv_sem=ex_recv.at[n, 1],
            device_id=(dp, d), device_id_type=MESH,
        )
        return e, c

    def ex_start(n):
        for rel in PEERS:
            d = peer(rel)
            for copy in ex_copies(n, d, me, d):
                copy.start()
        r_edge[n, me] = s_edge[n, me]
        r_corner[n, me] = s_corner[n, me]

    def ex_all(n):
        rest = pl.ds(0, N_TILE - 1)
        return ex_copies(n, rest, rest, peer(OFFSETS[0]))

    def ex_wait(n):
        for copy in ex_all(n):
            copy.wait_recv()
        return flat(r_edge[n]), flat(r_corner[n])

    gather(0, pad1)
    pl.semaphore_wait(barrier, N_TILE)
    ex_start(0)

    for load in loads[5:]:
        load.wait()
    ownb = own.astype(BF16)
    pick = hot(iota((128, 1), 0).astype(F32) + me_f * float(T) == lane_f)
    my_row = mm_nt(ownb, pick)
    my_col = mm_nt(pick[0:16], ownb)
    earlier = iota((T, 128), 1).astype(F32) < iota((T, 128), 0).astype(F32)

    def slot_base(kind, per_owner, per_rank):
        out = []
        for k in range(4 * kind, 4 * kind + 4):
            col = my_col[:, k:k + 1]
            shared = jnp.zeros((T, 128), F32)
            for k2 in range(4 * kind, 4 * kind + 4):
                shared = shared + jnp.where(col == my_row[k2:k2 + 1], 1.0, 0.0)
            rk = jnp.sum(jnp.where(earlier, shared, 0.0), axis=1, keepdims=True)
            out.append(col * per_owner + rk * per_rank)
        return out

    base_e = slot_base(0, 16.0, 8.0)
    base_c = slot_base(1, 2.0, 1.0)
    col_e = jnp.concatenate([b + float(px) for b in base_e for px in range(S)], axis=0)
    col_c = jnp.concatenate(base_c + [jnp.full((64, 1), -1.0, F32)], axis=0)
    r_mat[...] = hot(col_e == lane_f)
    rc_mat[...] = hot(col_c == lane_f[:, :128])

    def taps_sum(read, w):
        out = None
        for a in range(0, 9, 2):
            taps = TAPS[a:a + 2]
            lhs = [read(p, q) for p, q in taps]
            lhs = lhs[0] if len(lhs) == 1 else jnp.concatenate(lhs, axis=1)
            part = mm(lhs, w[a * C:(a + len(taps)) * C])
            out = part if out is None else out + part
        return out

    def conv_centre(pad, w, pre):
        for i in range(0, S, 2):
            v = taps_sum(lambda p, q: flat(pad[i + p:i + p + 2, q:q + 8]), w)
            pre[i:i + 2] = v.reshape(2, S, T, C)

    def first_act(region):
        v = pre1[region]
        pad2[moved(region, 1)] = (v * logistic(v)).astype(BF16)

    pad2[...] = jnp.zeros_like(pad2)
    slope_pad[...] = jnp.zeros_like(slope_pad)
    conv_centre(pad1, w1_ref, pre1)
    first_act(INSIDE)
    for tap in range(4):
        at = slice(tap * C, tap * C + C)
        wdt[at] = flip(wd_ref[at])
    small[...] = cot_ref[...].astype(F32)
    for px in range(16):
        cot_p[pl.ds(px * T, T), :] = small[pl.ds(px, T, stride=16), :].astype(BF16)
    for tap in range(4):
        back = mm(cot_p[...], wdt[tap * C:tap * C + C]).reshape(4, 4, T, C)
        back6[:, tap // 2, :, tap % 2] = back
    back2[...] = back6[...].reshape(S, S, T, C)
    for tap in range(9):
        at = slice(tap * C, tap * C + C)
        w2t[at] = flip(w2_ref[at])

    def fill_rims(n, pad):
        edges, corners = ex_wait(n)
        rims = mm(r_mat[...], edges).astype(BF16).reshape(4, S, T, C)
        at_corner = mm(rc_mat[...], corners).astype(BF16)
        pad[0, 1:9] = rims[0]
        pad[1:9, 9] = rims[1]
        pad[9, 1:9] = rims[2]
        pad[1:9, 0] = rims[3]
        pad[0, 9] = at_corner[0:16]
        pad[9, 9] = at_corner[16:32]
        pad[9, 0] = at_corner[32:48]
        pad[0, 0] = at_corner[48:64]

    def rim_taps(pad, w, pre):
        for i, row, p in ((0, 0, 0), (7, 9, 2)):
            lhs = jnp.concatenate([flat(pad[row, q:q + 8]) for q in range(3)], axis=1)
            pre[i] = pre[i] + cells(mm(lhs, w[3 * p * C:(3 * p + 3) * C]))
        zero = jnp.zeros((T, C), BF16)
        for j, col, q in ((0, 0, 0), (7, 9, 2)):
            lhs = [
                jnp.concatenate([zero, flat(pad[1:8, col])], axis=0),
                flat(pad[1:9, col]),
                jnp.concatenate([flat(pad[2:9, col]), zero], axis=0),
            ]
            part = None
            for p in range(3):
                one = mm(lhs[p], w[(3 * p + q) * C:(3 * p + q + 1) * C])
                part = one if part is None else part + one
            pre[:, j] = pre[:, j] + cells(part)

    fill_rims(0, pad1)
    rim_taps(pad1, w1_ref, pre1)
    for region in EDGE_LINES:
        first_act(region)
    gather(1, pad2)
    ex_start(1)

    conv_centre(pad2, w2_ref, pre2)

    def second_act(region):
        v = pre2[region]
        s = logistic(v)
        hid2[region] = (v * s).astype(BF16)
        slope_pad[moved(region, 2)] = (back2[region] * (s * (1.0 + v * (1.0 - s)))).astype(BF16)

    second_act(INSIDE)
    cot_t[...] = flip(cot_p[...])
    for tap in range(9):
        at = slice(tap * C, tap * C + C)
        w1t[at] = flip(w1_ref[at])
    row_e = jnp.transpose(jnp.broadcast_to(col_e, (512, 128)))[0:1]
    row_c = jnp.transpose(jnp.broadcast_to(col_c, (128, 128)))[0:1]
    rt_mat[...] = hot(sub_f == row_e)
    rct_mat[...] = hot(sub_f[:128] == row_c)
    gt_mat[...] = hot(sub_f[:512] == te)
    gct_mat[...] = hot(sub_f[:512] == tc)

    def return_rims(n, wt):
        rows = []
        for row, p in ((2, 0), (9, 2)):
            lhs = jnp.concatenate([flat(slope_pad[row, 2 - q:12 - q]) for q in range(3)], axis=1)
            rows.append(mm(lhs, wt[3 * p * C:(3 * p + 3) * C]).astype(BF16))
        cols = []
        for col, q in ((2, 0), (9, 2)):
            part = None
            for p in range(3):
                at = slice((3 * p + q) * C, (3 * p + q + 1) * C)
                one = mm(flat(slope_pad[3 - p:11 - p, col]), wt[at])
                part = one if part is None else part + one
            cols.append(part.astype(BF16))
        top, bottom = rows
        left, right = cols
        edges = jnp.concatenate([top[T:9 * T], right, bottom[T:9 * T], left], axis=0)
        corners = jnp.concatenate(
            [top[9 * T:], bottom[9 * T:], bottom[:T], top[:T], jnp.zeros((64, C), BF16)], axis=0
        )
        pack(n, mm(rt_mat[...], edges), mm(rct_mat[...], corners))
        ex_start(n)

    def back_centre(wt):
        for a in range(1, 9, 2):
            v = taps_sum(lambda p, q: flat(slope_pad[a + 2 - p:a + 4 - p, 3 - q:11 - q]), wt)
            inner[a - 1:a + 1] = v.reshape(2, S, T, C)

    def add_returned(n):
        edges, corners = ex_wait(n)
        lines = mm(gt_mat[...], edges) + mm(gct_mat[...], corners)
        lines = lines.reshape(4, S, T, C)
        inner[0] = inner[0] + lines[0]
        inner[7] = inner[7] + lines[1]
        inner[:, 0] = inner[:, 0] + lines[2]
        inner[:, 7] = inner[:, 7] + lines[3]

    fill_rims(1, pad2)
    rim_taps(pad2, w2_ref, pre2)
    for region in EDGE_LINES:
        second_act(region)
    return_rims(2, w2t)

    hid = hid2[...].reshape(4, 2, 4, 2, T, C)

    def hid_tap(tap):
        return flat(hid[:, tap // 2, :, tap % 2])

    def put(gf, tap, per_half, at, value, add=False):
        value = jnp.transpose(value).reshape(8, 16, C)
        low = tap * 8
        for half in range(2):
            lo, hi = max(low, half * per_half), min(low + 8, (half + 1) * per_half)
            if lo < hi:
                to = slice(at + lo - half * per_half, at + hi - half * per_half)
                part = value[lo - low:hi - low]
                gf[half, to] = gf[half, to] + part if add else part

    def weight_grad(slope_rows, read, gf, add=False):
        slope_t = flip(slope_rows)
        for a in range(0, 9, 2):
            taps = TAPS[a:a + 2]
            rhs = [read(p, q) for p, q in taps]
            rhs = rhs[0] if len(rhs) == 1 else jnp.concatenate(rhs, axis=1)
            both = mm(slope_t, rhs)
            for j in range(len(taps)):
                put(gf, a + j, 36, 0, both[:, j * C:(j + 1) * C], add)

    for tap in range(4):
        put(gf0, tap, 16, 36, mm(cot_t[...], hid_tap(tap)))
    weight_grad(
        flat(slope_pad[2:10, 2:10]), lambda p, q: flat(pad2[p:p + 8, q:q + 8]), gf0
    )

    late = ((gf0, s_a0, r_a0, r_c0), (gf1, s_a1, r_a1, r_c1))

    def owned(n, tile):
        nb = BLOCKS[n]
        b = lax.div(tile * nb + N_TILE - 1, N_TILE)
        return b, lax.div(b * N_TILE, nb) == tile

    def to_other_core(n, src_ref, dst_ref, stage):
        return pltpu.make_async_remote_copy(
            src_ref=src_ref, dst_ref=dst_ref,
            send_sem=red_send.at[n, stage], recv_sem=red_recv.at[n, stage],
            device_id=(dp, me + 1 - 2 * core), device_id_type=MESH,
        )

    def many(n, stage, count):
        at = pl.ds(0, count)
        return to_other_core(n, s_b.at[n, at], r_b.at[n, at], stage)

    def swap(n):
        return to_other_core(n, late[n][1], late[n][2], 0)

    def swap_start(n):
        gf, s_a = late[n][:2]
        s_a[...] = (gf[1 - core] * GRAD_SCALE).astype(BF16)
        swap(n).start()

    def scatter_start(n):
        gf, _, r_a, _ = late[n]
        swap(n).wait_recv()
        s_b[n, 0:BLOCKS[n]] = (gf[core] * GRAD_SCALE + r_a[...].astype(F32)).astype(BF16)
        for rel in OFFSETS:
            tile = peer(rel)
            b, owns = owned(n, tile)
            if rel == (0, 0, 0, 0):
                @pl.when(jnp.logical_and(owns, dp == core))
                def _():
                    r_b[n, chip] = s_b[n, b]

                owns = jnp.logical_and(owns, dp != core)

            @pl.when(owns)
            def _():
                pltpu.make_async_remote_copy(
                    src_ref=s_b.at[n, b], dst_ref=r_b.at[n, chip],
                    send_sem=red_send.at[n, 1], recv_sem=red_recv.at[n, 1],
                    device_id=(core, tile), device_id_type=MESH,
                ).start()

    def share_start(n):
        b, owns = owned(n, me)

        @pl.when(owns)
        def _():
            @pl.when(dp == core)
            def _():
                many(n, 1, 63).wait_recv()

            @pl.when(dp != core)
            def _():
                many(n, 1, 64).wait_recv()

            s_c[n] = jnp.sum(r_b[n].astype(F32), axis=0).astype(BF16)
            for rel in PEERS:
                pltpu.make_async_remote_copy(
                    src_ref=s_c.at[n], dst_ref=late[n][3].at[b],
                    send_sem=red_send.at[n, 2], recv_sem=red_recv.at[n, 2],
                    device_id=(dp, peer(rel)), device_id_type=MESH,
                ).start()
            late[n][3][b] = s_c[n]

    def share_wait(n):
        b, owns = owned(n, me)

        @pl.when(owns)
        def _():
            many(n, 2, BLOCKS[n] - 1).wait_recv()

        @pl.when(jnp.logical_not(owns))
        def _():
            many(n, 2, BLOCKS[n]).wait_recv()

    swap_start(0)
    back_centre(w2t)
    scatter_start(0)
    feats = None
    for tap in range(4):
        part = mm(hid_tap(tap), wd_ref[tap * C:tap * C + C])
        feats = part if feats is None else feats + part
    feat_ref[...] = feats

    def first_slope(region):
        slope_pad[moved(region, 2)] = (inner[region] * silu_slope(pre1[region])).astype(BF16)

    first_slope(INSIDE)
    weight_grad(
        flat(slope_pad[3:9, 3:9]), lambda p, q: flat(pad1[1 + p:7 + p, 1 + q:7 + q]), gf1
    )

    def edge_cells(ref, p, q):
        lines = [ref[p, q:q + 8], ref[7 + p, q:q + 8], ref[1 + p:7 + p, q], ref[1 + p:7 + p, 7 + q]]
        return jnp.concatenate([flat(v) for v in lines], axis=0)

    add_returned(2)
    for region in EDGE_LINES:
        first_slope(region)
    weight_grad(edge_cells(slope_pad, 2, 2), lambda p, q: edge_cells(pad1, p, q), gf1, add=True)
    swap_start(1)
    return_rims(3, w1t)
    scatter_start(1)
    share_start(0)
    back_centre(w1t)
    share_start(1)
    add_returned(3)
    ig_ref[...] = flat(inner[...])
    share_wait(0)
    late0_ref[...] = r_c0[...]
    share_wait(1)
    late1_ref[...] = r_c1[...]

    for n in range(4):
        for copy in ex_all(n):
            copy.wait_send()
    for n in range(2):
        nb = BLOCKS[n]
        swap(n).wait_send()
        b, owns = owned(n, me)
        kept = jnp.logical_and(owns, dp == core)

        @pl.when(kept)
        def _():
            many(n, 1, nb - 1).wait_send()

        @pl.when(jnp.logical_not(kept))
        def _():
            many(n, 1, nb).wait_send()

        @pl.when(owns)
        def _():
            many(n, 2, N_TILE - 1).wait_send()


def finish(feat_in, ig_in, late0, late1, feat_ref, ig_ref, o1_ref, o2_ref, od_ref):
    for t in range(T):
        feat_ref[pl.ds(t * 16, 16), :] = feat_in[pl.ds(t, 16, stride=T), :].astype(BF16)
        ig_ref[pl.ds(t * 64, 64), :] = ig_in[pl.ds(t, 64, stride=T), :]
    o1_ref[...] = flat(late1[...].astype(F32))
    o2_ref[...] = flat(late0[0:36].astype(F32))
    od_ref[...] = flat(late0[36:52].astype(F32))


def local(inputs, cotangent, w_first, w_second, w_down, edge_owner, corner_owner, neighbour_tile, seam_rotation):
    vmem = pl.BlockSpec(memory_space=pltpu.VMEM)
    v = pltpu.VMEM
    shape = jax.ShapeDtypeStruct
    between = pl.pallas_call(
        kernel,
        out_shape=(
            shape((256, C), F32), shape((1024, C), F32), shape((52, 16, C), BF16), shape((36, 16, C), BF16),
        ),
        in_specs=[pl.BlockSpec(memory_space=pltpu.HBM)] * 9,
        out_specs=(vmem,) * 4,
        scratch_shapes=[
            v((1024, C), BF16),
            v((256, C), BF16),
            v((1152, C), BF16),
            v((1152, C), BF16),
            v((512, C), BF16),
            v((4, 1024), jnp.int32),
            v((4, 1024), jnp.int32),
            v((8, 1024), jnp.int32),
            v((8, 1024), jnp.int32),
            v((1024, C), F32),
            v((S, S, T, C), F32),
            v((S, S, T, C), F32),
            v((S, S, T, C), F32),
            v((10, 10, T, C), BF16),
            v((10, 10, T, C), BF16),
            v((12, 12, T, C), BF16),
            v((1024, 512), BF16),
            v((512, 1024), BF16),
            v((128, 512), BF16),
            v((512, 128), BF16),
            v((512, 1024), BF16),
            v((1024, 512), BF16),
            v((128, 128), BF16),
            v((128, 128), BF16),
            v((1152, C), BF16),
            v((1152, C), BF16),
            v((512, C), BF16),
            v((4, 2, 4, 2, T, C), F32),
            v((S, S, T, C), F32),
            v((S, S, T, C), BF16),
            v((256, C), BF16),
            v((C, 256), BF16),
            v((256, C), F32),
            v((2, 52, 16, C), F32),
            v((2, 36, 16, C), F32),
            v((52, 16, C), BF16),
            v((36, 16, C), BF16),
            v((52, 16, C), BF16),
            v((36, 16, C), BF16),
            v((2, 64, 16, C), BF16),
            v((2, 64, 16, C), BF16),
            v((2, 16, C), BF16),
            v((52, 16, C), BF16),
            v((36, 16, C), BF16),
            v((4, N_TILE, T, C), BF16),
            v((4, N_TILE, T, C), BF16),
            v((4, N_TILE, 2, C), BF16),
            v((4, N_TILE, 2, C), BF16),
            pltpu.SemaphoreType.DMA((9,)),
            pltpu.SemaphoreType.DMA((4, 2)),
            pltpu.SemaphoreType.DMA((4, 2)),
            pltpu.SemaphoreType.DMA((2, 3)),
            pltpu.SemaphoreType.DMA((2, 3)),
        ],
        compiler_params=pltpu.CompilerParams(
            collective_id=0, has_side_effects=True, vmem_limit_bytes=32 * 1024 * 1024
        ),
    )(
        *[
            pltpu.with_memory_space_constraint(a, pltpu.HBM)
            for a in (
                inputs.reshape(1024, C), cotangent.reshape(256, C), w_first, w_second, w_down,
                edge_owner.T, corner_owner.T, neighbour_tile.T, seam_rotation.T,
            )
        ]
    )
    feats, grads, one, two, low = pl.pallas_call(
        finish,
        out_shape=(
            shape((256, C), BF16), shape((1024, C), F32), shape((576, C), F32),
            shape((576, C), F32), shape((256, C), F32),
        ),
        in_specs=[vmem] * 4,
        out_specs=(vmem,) * 5,
        compiler_params=pltpu.CompilerParams(vmem_limit_bytes=16 * 1024 * 1024),
    )(*between)
    return (feats.reshape(1, T, 4, 4, C), grads.reshape(1, T, S, S, C), one, two, low)


def solution(mesh):
    tiles = P("dp", "tile", None, None, None)
    return jax.shard_map(
        local,
        mesh=mesh,
        in_specs=(tiles, tiles) + (P(),) * 7,
        out_specs=(tiles, tiles) + (P("dp", None),) * 3,
        check_vma=False,
    )
```

```python
import itertools

import jax
import jax.numpy as jnp
import numpy as np
from jax import lax
from jax.experimental import pallas as pl
from jax.experimental.pallas import tpu as pltpu
from jax.sharding import PartitionSpec as P

MESH = pl.DeviceIdType.MESH
F32 = jnp.float32
BF16 = jnp.bfloat16
N_TILE = 64
T = 16
S = 8
C = 128
PIX = S * S * T
TAPS = [(p, q) for p in range(3) for q in range(3)]
GRAD_SCALE = float(2 * 1024 * 64) ** -0.5
BLOCKS = (36 + 16, 36)


def hops(rel):
    return min(rel[0], 4 - rel[0]) + rel[1] + min(rel[2], 4 - rel[2]) + 0.3 * rel[3]


OFFSETS = sorted(itertools.product(range(4), range(2), range(4), range(2)), key=hops, reverse=True)
PEERS = OFFSETS[:-1]
EDGE_LINES = [(0, slice(0, 8)), (7, slice(0, 8)), (slice(1, 7), 0), (slice(1, 7), 7)]
INSIDE = (slice(1, 7), slice(1, 7))


def seam_lines():
    grid = np.arange(S * S).reshape(S, S)
    sides = [grid[0], grid[-1], grid[:, 0], grid[:, -1]]
    first = np.zeros((8, 4), int)
    step = np.zeros((8, 4), int)
    for turn in range(4):
        turned = np.rot90(grid, turn)
        lines = [turned[-1, :], turned[:, 0], turned[0, :], turned[:, -1]]
        for k, line in enumerate(lines):
            for n, side in enumerate(sides):
                if (line == side).all():
                    first[k, turn], step[k, turn] = 8 * n, 1
                if (line[::-1] == side).all():
                    first[k, turn], step[k, turn] = 8 * n + 7, -1
        cells = [turned[-1, 0], turned[0, 0], turned[0, -1], turned[-1, -1]]
        for k, cell in enumerate(cells):
            first[4 + k, turn] = {0: 0, 7: 7, 56: 8, 63: 15}[int(cell)]
    return first, step


def iota(shape, axis):
    return lax.broadcasted_iota(jnp.int32, shape, axis)


def hot(mask):
    return jnp.where(mask, 1.0, 0.0).astype(BF16)


def mm(a, b):
    return jnp.dot(a, b, preferred_element_type=F32)


def mm_nt(a, b):
    return lax.dot_general(a, b, (((1,), (1,)), ((), ())), preferred_element_type=F32)


def logistic(v):
    return 1.0 / (1.0 + jnp.exp(-v))


def silu_slope(v):
    s = logistic(v)
    return s * (1.0 + v * (1.0 - s))


def flip(w):
    return jnp.transpose(w.astype(F32)).astype(BF16)


def flat(v):
    return v.reshape(-1, C)


def cells(v):
    return v.reshape(-1, T, C)


def moved(region, by):
    return tuple(slice(r.start + by, r.stop + by) if isinstance(r, slice) else r + by for r in region)


def kernel(
    x_hbm, cot_hbm, w1_hbm, w2_hbm, wd_hbm, eo_hbm, co_hbm, nb_hbm, rot_hbm,
    feat_ref, ig_ref, late0_ref, late1_ref,
    x_ref, cot_ref, w1_ref, w2_ref, wd_ref, eo_ref, co_ref, nb_ref, rot_ref,
    wide, inner, pre1, pre2, pad1, pad2, slope_pad, g_mat, gt_mat, gc_mat, gct_mat,
    r_mat, rt_mat, rc_mat, rct_mat, w1t, w2t, wdt, back6, back2, hid2, cot_p, cot_t,
    small, gf0, gf1, s_a0, s_a1, r_a0, r_a1, s_b, r_b, s_c, r_c0, r_c1,
    s_edge, r_edge, s_corner, r_corner,
    load_sem, ex_send, ex_recv, red_send, red_recv,
):
    dp = lax.axis_index("dp")
    me = lax.axis_index("tile")
    core = lax.rem(me, 2)
    chip = dp * 32 + lax.div(me, 2)
    at_x = [lax.rem(lax.div(me, 16) + d, 4) * 16 for d in range(4)]
    at_z = [lax.rem(lax.div(me, 8) + d, 2) * 8 for d in range(2)]
    at_y = [lax.rem(lax.div(me, 2) + d, 4) * 2 for d in range(4)]
    at_c = [lax.rem(me + d, 2) for d in range(2)]

    def peer(rel):
        return at_x[rel[0]] + at_z[rel[1]] + at_y[rel[2]] + at_c[rel[3]]

    pairs = [
        (eo_hbm, eo_ref), (co_hbm, co_ref), (nb_hbm, nb_ref), (rot_hbm, rot_ref), (x_hbm, x_ref),
        (cot_hbm, cot_ref), (w1_hbm, w1_ref), (w2_hbm, w2_ref), (wd_hbm, wd_ref),
    ]
    loads = [pltpu.make_async_copy(a, b, load_sem.at[i]) for i, (a, b) in enumerate(pairs)]
    for load in loads:
        load.start()
    barrier = pltpu.get_barrier_semaphore()
    pl.semaphore_signal(barrier, inc=1, device_id=(1 - dp, me), device_id_type=MESH)
    for rel in PEERS:
        pl.semaphore_signal(barrier, inc=1, device_id=(dp, peer(rel)), device_id_type=MESH)
    for load in loads[:4]:
        load.wait()

    me_f = me.astype(F32)
    own = jnp.concatenate([eo_ref[...], co_ref[...]], axis=0).astype(F32)
    src = nb_ref[...].astype(F32)
    rot = rot_ref[...].astype(F32)
    row8 = iota((8, 1024), 0)
    first, step = seam_lines()
    base_v = jnp.zeros((8, 1024), F32)
    step_v = jnp.zeros((8, 1024), F32)
    for turn in range(4):
        bcol = jnp.zeros((8, 1024), F32)
        scol = jnp.zeros((8, 1024), F32)
        for k in range(8):
            bcol = jnp.where(row8 == k, float(first[k, turn]), bcol)
            scol = jnp.where(row8 == k, float(step[k, turn]), scol)
        base_v = jnp.where(rot == float(turn), bcol, base_v)
        step_v = jnp.where(rot == float(turn), scol, step_v)
    match = jnp.where(own == me_f, 1.0, 0.0)

    def per_kind(v):
        a = jnp.broadcast_to(jnp.sum(v[0:4], axis=0, keepdims=True), (4, 1024))
        b = jnp.broadcast_to(jnp.sum(v[4:8], axis=0, keepdims=True), (4, 1024))
        return jnp.concatenate([a, b], axis=0)

    has = per_kind(match)
    lane16 = jnp.bitwise_and(iota((8, 1024), 1), 15)
    acc = has
    for sh in (1, 2, 4, 8):
        acc = acc + jnp.where(lane16 >= sh, pltpu.roll(acc, sh, 1), 0.0)
    rank = acc - has
    table = []
    for s in range(2):
        sel = match * jnp.where(rank == float(s), 1.0, 0.0)
        for v in (sel, sel * base_v, sel * step_v, sel * src):
            table.append(per_kind(v))
    tab = jnp.concatenate([v[0:1] for v in table] + [v[4:5] for v in table], axis=0).astype(BF16)
    lane_i = iota((1, 1024), 1)
    sub_i = iota((1024, 1), 0)
    lane_f = lane_i.astype(F32)
    sub_f = sub_i.astype(F32)
    blk_l = jnp.right_shift(lane_i, 4).astype(F32)
    blk_s = jnp.right_shift(sub_i, 4).astype(F32)
    block_diag = hot(blk_s == blk_l)
    slots_e = mm(tab, block_diag)
    pair_s = jnp.right_shift(iota((128, 1), 0), 1).astype(F32)
    slots_c = mm_nt(tab, hot(pair_s == blk_l))

    def target(rows, which, px):
        v0, b0, t0, n0, v1, b1, t1, n1 = [rows[i:i + 1] for i in range(8)]
        late = which > 0.5
        valid = jnp.where(late, v1, v0)
        line = jnp.where(late, b1, b0) + jnp.where(late, t1, t0) * px
        return jnp.where(valid > 0.5, line * float(T) + jnp.where(late, n1, n0), -1.0)

    te = target(
        slots_e[0:8],
        jnp.bitwise_and(jnp.right_shift(lane_i, 3), 1).astype(F32),
        jnp.bitwise_and(lane_i, 7).astype(F32),
    )
    tc = target(slots_c[8:16], jnp.bitwise_and(lane_i[:, :128], 1).astype(F32), 0.0)

    def as_column(row, n):
        return jnp.transpose(jnp.broadcast_to(row, (128, n)))[:, 0:1]

    g_mat[...] = hot(as_column(te, 1024) == lane_f[:, :512])
    gc_mat[...] = hot(as_column(tc, 128) == lane_f[:, :512])

    pad1[...] = jnp.zeros_like(pad1)
    loads[4].wait()
    wide[...] = x_ref[...].astype(F32)
    for px in range(S * S):
        pad1[1 + px // S, 1 + px % S] = wide[pl.ds(px, T, stride=S * S), :].astype(BF16)

    def pack(n, edges, corners):
        s_edge[n] = edges.astype(BF16).reshape(N_TILE, T, C)
        s_corner[n] = corners.astype(BF16).reshape(N_TILE, 2, C)

    def gather(n, pad):
        lines = [pad[1, 1:9], pad[8, 1:9], pad[1:9, 1], pad[1:9, 8]]
        lines = jnp.concatenate([flat(v) for v in lines], axis=0)
        pack(n, mm(g_mat[...], lines), mm(gc_mat[...], lines))

    def ex_copies(n, src_at, dst_at, d):
        e = pltpu.make_async_remote_copy(
            src_ref=s_edge.at[n, src_at], dst_ref=r_edge.at[n, dst_at],
            send_sem=ex_send.at[n, 0], recv_sem=ex_recv.at[n, 0],
            device_id=(dp, d), device_id_type=MESH,
        )
        c = pltpu.make_async_remote_copy(
            src_ref=s_corner.at[n, src_at], dst_ref=r_corner.at[n, dst_at],
            send_sem=ex_send.at[n, 1], recv_sem=ex_recv.at[n, 1],
            device_id=(dp, d), device_id_type=MESH,
        )
        return e, c

    def ex_start(n):
        for rel in PEERS:
            d = peer(rel)
            for copy in ex_copies(n, d, me, d):
                copy.start()
        r_edge[n, me] = s_edge[n, me]
        r_corner[n, me] = s_corner[n, me]

    def ex_all(n):
        rest = pl.ds(0, N_TILE - 1)
        return ex_copies(n, rest, rest, peer(OFFSETS[0]))

    def ex_wait(n):
        for copy in ex_all(n):
            copy.wait_recv()
        return flat(r_edge[n]), flat(r_corner[n])

    gather(0, pad1)
    pl.semaphore_wait(barrier, N_TILE)
    ex_start(0)

    for load in loads[5:]:
        load.wait()
    ownb = own.astype(BF16)
    pick = hot(iota((128, 1), 0).astype(F32) + me_f * float(T) == lane_f)
    my_row = mm_nt(ownb, pick)
    my_col = mm_nt(pick[0:16], ownb)
    earlier = iota((T, 128), 1).astype(F32) < iota((T, 128), 0).astype(F32)

    def slot_base(kind, per_owner, per_rank):
        out = []
        for k in range(4 * kind, 4 * kind + 4):
            col = my_col[:, k:k + 1]
            shared = jnp.zeros((T, 128), F32)
            for k2 in range(4 * kind, 4 * kind + 4):
                shared = shared + jnp.where(col == my_row[k2:k2 + 1], 1.0, 0.0)
            rk = jnp.sum(jnp.where(earlier, shared, 0.0), axis=1, keepdims=True)
            out.append(col * per_owner + rk * per_rank)
        return out

    base_e = slot_base(0, 16.0, 8.0)
    base_c = slot_base(1, 2.0, 1.0)
    col_e = jnp.concatenate([b + float(px) for b in base_e for px in range(S)], axis=0)
    col_c = jnp.concatenate(base_c + [jnp.full((64, 1), -1.0, F32)], axis=0)
    r_mat[...] = hot(col_e == lane_f)
    rc_mat[...] = hot(col_c == lane_f[:, :128])

    def taps_sum(read, w):
        out = None
        for a in range(0, 9, 2):
            taps = TAPS[a:a + 2]
            lhs = [read(p, q) for p, q in taps]
            lhs = lhs[0] if len(lhs) == 1 else jnp.concatenate(lhs, axis=1)
            part = mm(lhs, w[a * C:(a + len(taps)) * C])
            out = part if out is None else out + part
        return out

    def conv_centre(pad, w, pre):
        for i in range(0, S, 2):
            v = taps_sum(lambda p, q: flat(pad[i + p:i + p + 2, q:q + 8]), w)
            pre[i:i + 2] = v.reshape(2, S, T, C)

    def first_act(region):
        v = pre1[region]
        pad2[moved(region, 1)] = (v * logistic(v)).astype(BF16)

    pad2[...] = jnp.zeros_like(pad2)
    slope_pad[...] = jnp.zeros_like(slope_pad)
    conv_centre(pad1, w1_ref, pre1)
    first_act(INSIDE)
    for tap in range(4):
        at = slice(tap * C, tap * C + C)
        wdt[at] = flip(wd_ref[at])
    small[...] = cot_ref[...].astype(F32)
    for px in range(16):
        cot_p[pl.ds(px * T, T), :] = small[pl.ds(px, T, stride=16), :].astype(BF16)
    for tap in range(4):
        back = mm(cot_p[...], wdt[tap * C:tap * C + C]).reshape(4, 4, T, C)
        back6[:, tap // 2, :, tap % 2] = back
    back2[...] = back6[...].reshape(S, S, T, C)
    for tap in range(9):
        at = slice(tap * C, tap * C + C)
        w2t[at] = flip(w2_ref[at])

    def fill_rims(n, pad):
        edges, corners = ex_wait(n)
        rims = mm(r_mat[...], edges).astype(BF16).reshape(4, S, T, C)
        at_corner = mm(rc_mat[...], corners).astype(BF16)
        pad[0, 1:9] = rims[0]
        pad[1:9, 9] = rims[1]
        pad[9, 1:9] = rims[2]
        pad[1:9, 0] = rims[3]
        pad[0, 9] = at_corner[0:16]
        pad[9, 9] = at_corner[16:32]
        pad[9, 0] = at_corner[32:48]
        pad[0, 0] = at_corner[48:64]

    def rim_taps(pad, w, pre):
        for i, row, p in ((0, 0, 0), (7, 9, 2)):
            lhs = jnp.concatenate([flat(pad[row, q:q + 8]) for q in range(3)], axis=1)
            pre[i] = pre[i] + cells(mm(lhs, w[3 * p * C:(3 * p + 3) * C]))
        zero = jnp.zeros((T, C), BF16)
        for j, col, q in ((0, 0, 0), (7, 9, 2)):
            lhs = [
                jnp.concatenate([zero, flat(pad[1:8, col])], axis=0),
                flat(pad[1:9, col]),
                jnp.concatenate([flat(pad[2:9, col]), zero], axis=0),
            ]
            part = None
            for p in range(3):
                one = mm(lhs[p], w[(3 * p + q) * C:(3 * p + q + 1) * C])
                part = one if part is None else part + one
            pre[:, j] = pre[:, j] + cells(part)

    fill_rims(0, pad1)
    rim_taps(pad1, w1_ref, pre1)
    for region in EDGE_LINES:
        first_act(region)
    gather(1, pad2)
    ex_start(1)

    conv_centre(pad2, w2_ref, pre2)

    def second_act(region):
        v = pre2[region]
        s = logistic(v)
        hid2[region] = (v * s).astype(BF16)
        slope_pad[moved(region, 2)] = (back2[region] * (s * (1.0 + v * (1.0 - s)))).astype(BF16)

    second_act(INSIDE)
    cot_t[...] = flip(cot_p[...])
    for tap in range(9):
        at = slice(tap * C, tap * C + C)
        w1t[at] = flip(w1_ref[at])
    row_e = jnp.transpose(jnp.broadcast_to(col_e, (512, 128)))[0:1]
    row_c = jnp.transpose(jnp.broadcast_to(col_c, (128, 128)))[0:1]
    rt_mat[...] = hot(sub_f == row_e)
    rct_mat[...] = hot(sub_f[:128] == row_c)
    gt_mat[...] = hot(sub_f[:512] == te)
    gct_mat[...] = hot(sub_f[:512] == tc)

    def return_rims(n, wt):
        rows = []
        for row, p in ((2, 0), (9, 2)):
            lhs = jnp.concatenate([flat(slope_pad[row, 2 - q:12 - q]) for q in range(3)], axis=1)
            rows.append(mm(lhs, wt[3 * p * C:(3 * p + 3) * C]).astype(BF16))
        cols = []
        for col, q in ((2, 0), (9, 2)):
            part = None
            for p in range(3):
                at = slice((3 * p + q) * C, (3 * p + q + 1) * C)
                one = mm(flat(slope_pad[3 - p:11 - p, col]), wt[at])
                part = one if part is None else part + one
            cols.append(part.astype(BF16))
        top, bottom = rows
        left, right = cols
        edges = jnp.concatenate([top[T:9 * T], right, bottom[T:9 * T], left], axis=0)
        corners = jnp.concatenate(
            [top[9 * T:], bottom[9 * T:], bottom[:T], top[:T], jnp.zeros((64, C), BF16)], axis=0
        )
        pack(n, mm(rt_mat[...], edges), mm(rct_mat[...], corners))

    def back_centre(wt):
        for a in range(1, 9, 2):
            v = taps_sum(lambda p, q: flat(slope_pad[a + 2 - p:a + 4 - p, 3 - q:11 - q]), wt)
            inner[a - 1:a + 1] = v.reshape(2, S, T, C)

    def add_returned(n):
        edges, corners = ex_wait(n)
        lines = mm(gt_mat[...], edges) + mm(gct_mat[...], corners)
        lines = lines.reshape(4, S, T, C)
        inner[0] = inner[0] + lines[0]
        inner[7] = inner[7] + lines[1]
        inner[:, 0] = inner[:, 0] + lines[2]
        inner[:, 7] = inner[:, 7] + lines[3]

    fill_rims(1, pad2)
    rim_taps(pad2, w2_ref, pre2)
    for region in EDGE_LINES:
        second_act(region)
    return_rims(2, w2t)
    ex_start(2)

    hid = hid2[...].reshape(4, 2, 4, 2, T, C)

    def hid_tap(tap):
        return flat(hid[:, tap // 2, :, tap % 2])

    def put(gf, tap, per_half, at, value, add=False):
        value = jnp.transpose(value).reshape(8, 16, C)
        low = tap * 8
        for half in range(2):
            lo, hi = max(low, half * per_half), min(low + 8, (half + 1) * per_half)
            if lo < hi:
                to = slice(at + lo - half * per_half, at + hi - half * per_half)
                part = value[lo - low:hi - low]
                gf[half, to] = gf[half, to] + part if add else part

    def weight_grad(slope_rows, read, gf, add=False):
        slope_t = flip(slope_rows)
        for a in range(0, 9, 2):
            taps = TAPS[a:a + 2]
            rhs = [read(p, q) for p, q in taps]
            rhs = rhs[0] if len(rhs) == 1 else jnp.concatenate(rhs, axis=1)
            both = mm(slope_t, rhs)
            for j in range(len(taps)):
                put(gf, a + j, 36, 0, both[:, j * C:(j + 1) * C], add)

    for tap in range(4):
        put(gf0, tap, 16, 36, mm(cot_t[...], hid_tap(tap)))
    weight_grad(
        flat(slope_pad[2:10, 2:10]), lambda p, q: flat(pad2[p:p + 8, q:q + 8]), gf0
    )

    late = ((gf0, s_a0, r_a0, r_c0), (gf1, s_a1, r_a1, r_c1))

    def owned(n, tile):
        nb = BLOCKS[n]
        b = lax.div(tile * nb + N_TILE - 1, N_TILE)
        return b, lax.div(b * N_TILE, nb) == tile

    def to_other_core(n, src_ref, dst_ref, stage):
        return pltpu.make_async_remote_copy(
            src_ref=src_ref, dst_ref=dst_ref,
            send_sem=red_send.at[n, stage], recv_sem=red_recv.at[n, stage],
            device_id=(dp, me + 1 - 2 * core), device_id_type=MESH,
        )

    def many(n, stage, count):
        at = pl.ds(0, count)
        return to_other_core(n, s_b.at[n, at], r_b.at[n, at], stage)

    def swap(n):
        return to_other_core(n, late[n][1], late[n][2], 0)

    def swap_start(n):
        gf, s_a = late[n][:2]
        s_a[...] = (gf[1 - core] * GRAD_SCALE).astype(BF16)
        swap(n).start()

    def scatter_start(n):
        gf, _, r_a, _ = late[n]
        swap(n).wait_recv()
        s_b[n, 0:BLOCKS[n]] = (gf[core] * GRAD_SCALE + r_a[...].astype(F32)).astype(BF16)
        for rel in OFFSETS:
            tile = peer(rel)
            b, owns = owned(n, tile)
            if rel == (0, 0, 0, 0):
                @pl.when(jnp.logical_and(owns, dp == core))
                def _():
                    r_b[n, chip] = s_b[n, b]

                owns = jnp.logical_and(owns, dp != core)

            @pl.when(owns)
            def _():
                pltpu.make_async_remote_copy(
                    src_ref=s_b.at[n, b], dst_ref=r_b.at[n, chip],
                    send_sem=red_send.at[n, 1], recv_sem=red_recv.at[n, 1],
                    device_id=(core, tile), device_id_type=MESH,
                ).start()

    def share_start(n):
        b, owns = owned(n, me)

        @pl.when(owns)
        def _():
            @pl.when(dp == core)
            def _():
                many(n, 1, 63).wait_recv()

            @pl.when(dp != core)
            def _():
                many(n, 1, 64).wait_recv()

            s_c[n] = jnp.sum(r_b[n].astype(F32), axis=0).astype(BF16)
            for rel in PEERS:
                pltpu.make_async_remote_copy(
                    src_ref=s_c.at[n], dst_ref=late[n][3].at[b],
                    send_sem=red_send.at[n, 2], recv_sem=red_recv.at[n, 2],
                    device_id=(dp, peer(rel)), device_id_type=MESH,
                ).start()
            late[n][3][b] = s_c[n]

    def share_wait(n):
        b, owns = owned(n, me)

        @pl.when(owns)
        def _():
            many(n, 2, BLOCKS[n] - 1).wait_recv()

        @pl.when(jnp.logical_not(owns))
        def _():
            many(n, 2, BLOCKS[n]).wait_recv()

    swap_start(0)
    back_centre(w2t)
    scatter_start(0)
    feats = None
    for tap in range(4):
        part = mm(hid_tap(tap), wd_ref[tap * C:tap * C + C])
        feats = part if feats is None else feats + part
    feat_ref[...] = feats

    def first_slope(region):
        slope_pad[moved(region, 2)] = (inner[region] * silu_slope(pre1[region])).astype(BF16)

    first_slope(INSIDE)
    weight_grad(
        flat(slope_pad[3:9, 3:9]), lambda p, q: flat(pad1[1 + p:7 + p, 1 + q:7 + q]), gf1
    )

    def edge_cells(ref, p, q):
        lines = [ref[p, q:q + 8], ref[7 + p, q:q + 8], ref[1 + p:7 + p, q], ref[1 + p:7 + p, 7 + q]]
        return jnp.concatenate([flat(v) for v in lines], axis=0)

    add_returned(2)
    for region in EDGE_LINES:
        first_slope(region)
    weight_grad(edge_cells(slope_pad, 2, 2), lambda p, q: edge_cells(pad1, p, q), gf1, add=True)
    swap_start(1)
    return_rims(3, w1t)
    scatter_start(1)
    back_centre(w1t)
    ex_start(3)
    share_start(0)
    share_start(1)
    add_returned(3)
    ig_ref[...] = flat(inner[...])
    share_wait(0)
    late0_ref[...] = r_c0[...]
    share_wait(1)
    late1_ref[...] = r_c1[...]

    for n in range(4):
        for copy in ex_all(n):
            copy.wait_send()
    for n in range(2):
        nb = BLOCKS[n]
        swap(n).wait_send()
        b, owns = owned(n, me)
        kept = jnp.logical_and(owns, dp == core)

        @pl.when(kept)
        def _():
            many(n, 1, nb - 1).wait_send()

        @pl.when(jnp.logical_not(kept))
        def _():
            many(n, 1, nb).wait_send()

        @pl.when(owns)
        def _():
            many(n, 2, N_TILE - 1).wait_send()


def finish(feat_in, ig_in, late0, late1, feat_ref, ig_ref, o1_ref, o2_ref, od_ref):
    for t in range(T):
        feat_ref[pl.ds(t * 16, 16), :] = feat_in[pl.ds(t, 16, stride=T), :].astype(BF16)
        ig_ref[pl.ds(t * 64, 64), :] = ig_in[pl.ds(t, 64, stride=T), :]
    o1_ref[...] = flat(late1[...].astype(F32))
    o2_ref[...] = flat(late0[0:36].astype(F32))
    od_ref[...] = flat(late0[36:52].astype(F32))


def local(inputs, cotangent, w_first, w_second, w_down, edge_owner, corner_owner, neighbour_tile, seam_rotation):
    vmem = pl.BlockSpec(memory_space=pltpu.VMEM)
    v = pltpu.VMEM
    shape = jax.ShapeDtypeStruct
    between = pl.pallas_call(
        kernel,
        out_shape=(
            shape((256, C), F32), shape((1024, C), F32), shape((52, 16, C), BF16), shape((36, 16, C), BF16),
        ),
        in_specs=[pl.BlockSpec(memory_space=pltpu.HBM)] * 9,
        out_specs=(vmem,) * 4,
        scratch_shapes=[
            v((1024, C), BF16),
            v((256, C), BF16),
            v((1152, C), BF16),
            v((1152, C), BF16),
            v((512, C), BF16),
            v((4, 1024), jnp.int32),
            v((4, 1024), jnp.int32),
            v((8, 1024), jnp.int32),
            v((8, 1024), jnp.int32),
            v((1024, C), F32),
            v((S, S, T, C), F32),
            v((S, S, T, C), F32),
            v((S, S, T, C), F32),
            v((10, 10, T, C), BF16),
            v((10, 10, T, C), BF16),
            v((12, 12, T, C), BF16),
            v((1024, 512), BF16),
            v((512, 1024), BF16),
            v((128, 512), BF16),
            v((512, 128), BF16),
            v((512, 1024), BF16),
            v((1024, 512), BF16),
            v((128, 128), BF16),
            v((128, 128), BF16),
            v((1152, C), BF16),
            v((1152, C), BF16),
            v((512, C), BF16),
            v((4, 2, 4, 2, T, C), F32),
            v((S, S, T, C), F32),
            v((S, S, T, C), BF16),
            v((256, C), BF16),
            v((C, 256), BF16),
            v((256, C), F32),
            v((2, 52, 16, C), F32),
            v((2, 36, 16, C), F32),
            v((52, 16, C), BF16),
            v((36, 16, C), BF16),
            v((52, 16, C), BF16),
            v((36, 16, C), BF16),
            v((2, 64, 16, C), BF16),
            v((2, 64, 16, C), BF16),
            v((2, 16, C), BF16),
            v((52, 16, C), BF16),
            v((36, 16, C), BF16),
            v((4, N_TILE, T, C), BF16),
            v((4, N_TILE, T, C), BF16),
            v((4, N_TILE, 2, C), BF16),
            v((4, N_TILE, 2, C), BF16),
            pltpu.SemaphoreType.DMA((9,)),
            pltpu.SemaphoreType.DMA((4, 2)),
            pltpu.SemaphoreType.DMA((4, 2)),
            pltpu.SemaphoreType.DMA((2, 3)),
            pltpu.SemaphoreType.DMA((2, 3)),
        ],
        compiler_params=pltpu.CompilerParams(
            collective_id=0, has_side_effects=True, vmem_limit_bytes=32 * 1024 * 1024
        ),
    )(
        *[
            pltpu.with_memory_space_constraint(a, pltpu.HBM)
            for a in (
                inputs.reshape(1024, C), cotangent.reshape(256, C), w_first, w_second, w_down,
                edge_owner.T, corner_owner.T, neighbour_tile.T, seam_rotation.T,
            )
        ]
    )
    feats, grads, one, two, low = pl.pallas_call(
        finish,
        out_shape=(
            shape((256, C), BF16), shape((1024, C), F32), shape((576, C), F32),
            shape((576, C), F32), shape((256, C), F32),
        ),
        in_specs=[vmem] * 4,
        out_specs=(vmem,) * 5,
        compiler_params=pltpu.CompilerParams(vmem_limit_bytes=16 * 1024 * 1024),
    )(*between)
    return (feats.reshape(1, T, 4, 4, C), grads.reshape(1, T, S, S, C), one, two, low)


def solution(mesh):
    tiles = P("dp", "tile", None, None, None)
    return jax.shard_map(
        local,
        mesh=mesh,
        in_specs=(tiles, tiles) + (P(),) * 7,
        out_specs=(tiles, tiles) + (P("dp", None),) * 3,
        check_vma=False,
    )
```

```python
import itertools

import jax
import jax.numpy as jnp
import numpy as np
from jax import lax
from jax.experimental import pallas as pl
from jax.experimental.pallas import tpu as pltpu
from jax.sharding import PartitionSpec as P

MESH = pl.DeviceIdType.MESH
F32 = jnp.float32
BF16 = jnp.bfloat16
N_TILE = 64
T = 16
S = 8
C = 128
PIX = S * S * T
TAPS = [(p, q) for p in range(3) for q in range(3)]
GRAD_SCALE = float(2 * 1024 * 64) ** -0.5
BLOCKS = (36 + 16, 36)


def hops(rel):
    return min(rel[0], 4 - rel[0]) + rel[1] + min(rel[2], 4 - rel[2]) + 0.3 * rel[3]


OFFSETS = sorted(itertools.product(range(4), range(2), range(4), range(2)), key=hops, reverse=True)
PEERS = OFFSETS[:-1]
EDGE_LINES = [(0, slice(0, 8)), (7, slice(0, 8)), (slice(1, 7), 0), (slice(1, 7), 7)]
INSIDE = (slice(1, 7), slice(1, 7))


def seam_lines():
    grid = np.arange(S * S).reshape(S, S)
    sides = [grid[0], grid[-1], grid[:, 0], grid[:, -1]]
    first = np.zeros((8, 4), int)
    step = np.zeros((8, 4), int)
    for turn in range(4):
        turned = np.rot90(grid, turn)
        lines = [turned[-1, :], turned[:, 0], turned[0, :], turned[:, -1]]
        for k, line in enumerate(lines):
            for n, side in enumerate(sides):
                if (line == side).all():
                    first[k, turn], step[k, turn] = 8 * n, 1
                if (line[::-1] == side).all():
                    first[k, turn], step[k, turn] = 8 * n + 7, -1
        cells = [turned[-1, 0], turned[0, 0], turned[0, -1], turned[-1, -1]]
        for k, cell in enumerate(cells):
            first[4 + k, turn] = {0: 0, 7: 7, 56: 8, 63: 15}[int(cell)]
    return first, step


def iota(shape, axis):
    return lax.broadcasted_iota(jnp.int32, shape, axis)


def hot(mask):
    return jnp.where(mask, 1.0, 0.0).astype(BF16)


def mm(a, b):
    return jnp.dot(a, b, preferred_element_type=F32)


def mm_nt(a, b):
    return lax.dot_general(a, b, (((1,), (1,)), ((), ())), preferred_element_type=F32)


def logistic(v):
    return 1.0 / (1.0 + jnp.exp(-v))


def silu_slope(v):
    s = logistic(v)
    return s * (1.0 + v * (1.0 - s))


def flip(w):
    return jnp.transpose(w.astype(F32)).astype(BF16)


def flat(v):
    return v.reshape(-1, C)


def cells(v):
    return v.reshape(-1, T, C)


def moved(region, by):
    return tuple(slice(r.start + by, r.stop + by) if isinstance(r, slice) else r + by for r in region)


def kernel(
    x_hbm, cot_hbm, w1_hbm, w2_hbm, wd_hbm, eo_hbm, co_hbm, nb_hbm, rot_hbm,
    feat_ref, ig_ref, late0_ref, late1_ref,
    x_ref, cot_ref, w1_ref, w2_ref, wd_ref, eo_ref, co_ref, nb_ref, rot_ref,
    wide, inner, pre1, pre2, pad1, pad2, slope_pad, g_mat, gt_mat, gc_mat, gct_mat,
    r_mat, rt_mat, rc_mat, rct_mat, w1t, w2t, wdt, back6, back2, hid2, cot_p, cot_t,
    small, patch_t, gf0, gf1, s_a0, s_a1, r_a0, r_a1, s_b, r_b, s_c, r_c0, r_c1,
    s_edge, r_edge, s_corner, r_corner,
    load_sem, ex_send, ex_recv, red_send, red_recv,
):
    dp = lax.axis_index("dp")
    me = lax.axis_index("tile")
    core = lax.rem(me, 2)
    chip = dp * 32 + lax.div(me, 2)
    at_x = [lax.rem(lax.div(me, 16) + d, 4) * 16 for d in range(4)]
    at_z = [lax.rem(lax.div(me, 8) + d, 2) * 8 for d in range(2)]
    at_y = [lax.rem(lax.div(me, 2) + d, 4) * 2 for d in range(4)]
    at_c = [lax.rem(me + d, 2) for d in range(2)]

    def peer(rel):
        return at_x[rel[0]] + at_z[rel[1]] + at_y[rel[2]] + at_c[rel[3]]

    pairs = [
        (eo_hbm, eo_ref), (co_hbm, co_ref), (nb_hbm, nb_ref), (rot_hbm, rot_ref), (x_hbm, x_ref),
        (cot_hbm, cot_ref), (w1_hbm, w1_ref), (w2_hbm, w2_ref), (wd_hbm, wd_ref),
    ]
    loads = [pltpu.make_async_copy(a, b, load_sem.at[i]) for i, (a, b) in enumerate(pairs)]
    for load in loads:
        load.start()
    barrier = pltpu.get_barrier_semaphore()
    pl.semaphore_signal(barrier, inc=1, device_id=(1 - dp, me), device_id_type=MESH)
    for rel in PEERS:
        pl.semaphore_signal(barrier, inc=1, device_id=(dp, peer(rel)), device_id_type=MESH)
    for load in loads[:4]:
        load.wait()

    me_f = me.astype(F32)
    own = jnp.concatenate([eo_ref[...], co_ref[...]], axis=0).astype(F32)
    src = nb_ref[...].astype(F32)
    rot = rot_ref[...].astype(F32)
    row8 = iota((8, 1024), 0)
    first, step = seam_lines()
    base_v = jnp.zeros((8, 1024), F32)
    step_v = jnp.zeros((8, 1024), F32)
    for turn in range(4):
        bcol = jnp.zeros((8, 1024), F32)
        scol = jnp.zeros((8, 1024), F32)
        for k in range(8):
            bcol = jnp.where(row8 == k, float(first[k, turn]), bcol)
            scol = jnp.where(row8 == k, float(step[k, turn]), scol)
        base_v = jnp.where(rot == float(turn), bcol, base_v)
        step_v = jnp.where(rot == float(turn), scol, step_v)
    match = jnp.where(own == me_f, 1.0, 0.0)

    def per_kind(v):
        a = jnp.broadcast_to(jnp.sum(v[0:4], axis=0, keepdims=True), (4, 1024))
        b = jnp.broadcast_to(jnp.sum(v[4:8], axis=0, keepdims=True), (4, 1024))
        return jnp.concatenate([a, b], axis=0)

    has = per_kind(match)
    lane16 = jnp.bitwise_and(iota((8, 1024), 1), 15)
    acc = has
    for sh in (1, 2, 4, 8):
        acc = acc + jnp.where(lane16 >= sh, pltpu.roll(acc, sh, 1), 0.0)
    rank = acc - has
    table = []
    for s in range(2):
        sel = match * jnp.where(rank == float(s), 1.0, 0.0)
        for v in (sel, sel * base_v, sel * step_v, sel * src):
            table.append(per_kind(v))
    tab = jnp.concatenate([v[0:1] for v in table] + [v[4:5] for v in table], axis=0).astype(BF16)
    lane_i = iota((1, 1024), 1)
    sub_i = iota((1024, 1), 0)
    lane_f = lane_i.astype(F32)
    sub_f = sub_i.astype(F32)
    blk_l = jnp.right_shift(lane_i, 4).astype(F32)
    blk_s = jnp.right_shift(sub_i, 4).astype(F32)
    block_diag = hot(blk_s == blk_l)
    slots_e = mm(tab, block_diag)
    pair_s = jnp.right_shift(iota((128, 1), 0), 1).astype(F32)
    slots_c = mm_nt(tab, hot(pair_s == blk_l))

    def target(rows, which, px):
        v0, b0, t0, n0, v1, b1, t1, n1 = [rows[i:i + 1] for i in range(8)]
        late = which > 0.5
        valid = jnp.where(late, v1, v0)
        line = jnp.where(late, b1, b0) + jnp.where(late, t1, t0) * px
        return jnp.where(valid > 0.5, line * float(T) + jnp.where(late, n1, n0), -1.0)

    te = target(
        slots_e[0:8],
        jnp.bitwise_and(jnp.right_shift(lane_i, 3), 1).astype(F32),
        jnp.bitwise_and(lane_i, 7).astype(F32),
    )
    tc = target(slots_c[8:16], jnp.bitwise_and(lane_i[:, :128], 1).astype(F32), 0.0)

    def as_column(row, n):
        return jnp.transpose(jnp.broadcast_to(row, (128, n)))[:, 0:1]

    g_mat[...] = hot(as_column(te, 1024) == lane_f[:, :512])
    gc_mat[...] = hot(as_column(tc, 128) == lane_f[:, :512])

    pad1[...] = jnp.zeros_like(pad1)
    loads[4].wait()
    wide[...] = x_ref[...].astype(F32)
    for px in range(S * S):
        pad1[1 + px // S, 1 + px % S] = wide[pl.ds(px, T, stride=S * S), :].astype(BF16)

    def pack(n, edges, corners):
        s_edge[n] = edges.astype(BF16).reshape(N_TILE, T, C)
        s_corner[n] = corners.astype(BF16).reshape(N_TILE, 2, C)

    def gather(n, pad):
        lines = [pad[1, 1:9], pad[8, 1:9], pad[1:9, 1], pad[1:9, 8]]
        lines = jnp.concatenate([flat(v) for v in lines], axis=0)
        pack(n, mm(g_mat[...], lines), mm(gc_mat[...], lines))

    def ex_copies(n, src_at, dst_at, d):
        e = pltpu.make_async_remote_copy(
            src_ref=s_edge.at[n, src_at], dst_ref=r_edge.at[n, dst_at],
            send_sem=ex_send.at[n, 0], recv_sem=ex_recv.at[n, 0],
            device_id=(dp, d), device_id_type=MESH,
        )
        c = pltpu.make_async_remote_copy(
            src_ref=s_corner.at[n, src_at], dst_ref=r_corner.at[n, dst_at],
            send_sem=ex_send.at[n, 1], recv_sem=ex_recv.at[n, 1],
            device_id=(dp, d), device_id_type=MESH,
        )
        return e, c

    def ex_start(n):
        for rel in PEERS:
            d = peer(rel)
            for copy in ex_copies(n, d, me, d):
                copy.start()
        r_edge[n, me] = s_edge[n, me]
        r_corner[n, me] = s_corner[n, me]

    def ex_all(n):
        rest = pl.ds(0, N_TILE - 1)
        return ex_copies(n, rest, rest, peer(OFFSETS[0]))

    def ex_wait(n):
        for copy in ex_all(n):
            copy.wait_recv()
        return flat(r_edge[n]), flat(r_corner[n])

    gather(0, pad1)
    pl.semaphore_wait(barrier, N_TILE)
    ex_start(0)

    for load in loads[5:]:
        load.wait()
    ownb = own.astype(BF16)
    pick = hot(iota((128, 1), 0).astype(F32) + me_f * float(T) == lane_f)
    my_row = mm_nt(ownb, pick)
    my_col = mm_nt(pick[0:16], ownb)
    earlier = iota((T, 128), 1).astype(F32) < iota((T, 128), 0).astype(F32)

    def slot_base(kind, per_owner, per_rank):
        out = []
        for k in range(4 * kind, 4 * kind + 4):
            col = my_col[:, k:k + 1]
            shared = jnp.zeros((T, 128), F32)
            for k2 in range(4 * kind, 4 * kind + 4):
                shared = shared + jnp.where(col == my_row[k2:k2 + 1], 1.0, 0.0)
            rk = jnp.sum(jnp.where(earlier, shared, 0.0), axis=1, keepdims=True)
            out.append(col * per_owner + rk * per_rank)
        return out

    base_e = slot_base(0, 16.0, 8.0)
    base_c = slot_base(1, 2.0, 1.0)
    col_e = jnp.concatenate([b + float(px) for b in base_e for px in range(S)], axis=0)
    col_c = jnp.concatenate(base_c + [jnp.full((64, 1), -1.0, F32)], axis=0)
    r_mat[...] = hot(col_e == lane_f)
    rc_mat[...] = hot(col_c == lane_f[:, :128])

    def taps_sum(read, w):
        out = None
        for a in range(0, 9, 2):
            taps = TAPS[a:a + 2]
            lhs = [read(p, q) for p, q in taps]
            lhs = lhs[0] if len(lhs) == 1 else jnp.concatenate(lhs, axis=1)
            part = mm(lhs, w[a * C:(a + len(taps)) * C])
            out = part if out is None else out + part
        return out

    def conv_centre(pad, w, pre):
        for i in range(0, S, 2):
            v = taps_sum(lambda p, q: flat(pad[i + p:i + p + 2, q:q + 8]), w)
            pre[i:i + 2] = v.reshape(2, S, T, C)

    def first_act(region):
        v = pre1[region]
        pad2[moved(region, 1)] = (v * logistic(v)).astype(BF16)

    pad2[...] = jnp.zeros_like(pad2)
    slope_pad[...] = jnp.zeros_like(slope_pad)
    conv_centre(pad1, w1_ref, pre1)
    first_act(INSIDE)
    for tap in range(4):
        at = slice(tap * C, tap * C + C)
        wdt[at] = flip(wd_ref[at])
    small[...] = cot_ref[...].astype(F32)
    for px in range(16):
        cot_p[pl.ds(px * T, T), :] = small[pl.ds(px, T, stride=16), :].astype(BF16)
    for tap in range(4):
        back = mm(cot_p[...], wdt[tap * C:tap * C + C]).reshape(4, 4, T, C)
        back6[:, tap // 2, :, tap % 2] = back
    back2[...] = back6[...].reshape(S, S, T, C)
    for tap in range(9):
        at = slice(tap * C, tap * C + C)
        w2t[at] = flip(w2_ref[at])

    def fill_rims(n, pad):
        edges, corners = ex_wait(n)
        rims = mm(r_mat[...], edges).astype(BF16).reshape(4, S, T, C)
        at_corner = mm(rc_mat[...], corners).astype(BF16)
        pad[0, 1:9] = rims[0]
        pad[1:9, 9] = rims[1]
        pad[9, 1:9] = rims[2]
        pad[1:9, 0] = rims[3]
        pad[0, 9] = at_corner[0:16]
        pad[9, 9] = at_corner[16:32]
        pad[9, 0] = at_corner[32:48]
        pad[0, 0] = at_corner[48:64]

    def rim_taps(pad, w, pre):
        for i, row, p in ((0, 0, 0), (7, 9, 2)):
            lhs = jnp.concatenate([flat(pad[row, q:q + 8]) for q in range(3)], axis=1)
            pre[i] = pre[i] + cells(mm(lhs, w[3 * p * C:(3 * p + 3) * C]))
        zero = jnp.zeros((T, C), BF16)
        for j, col, q in ((0, 0, 0), (7, 9, 2)):
            lhs = [
                jnp.concatenate([zero, flat(pad[1:8, col])], axis=0),
                flat(pad[1:9, col]),
                jnp.concatenate([flat(pad[2:9, col]), zero], axis=0),
            ]
            part = None
            for p in range(3):
                one = mm(lhs[p], w[(3 * p + q) * C:(3 * p + q + 1) * C])
                part = one if part is None else part + one
            pre[:, j] = pre[:, j] + cells(part)

    fill_rims(0, pad1)
    rim_taps(pad1, w1_ref, pre1)
    for region in EDGE_LINES:
        first_act(region)
    gather(1, pad2)
    ex_start(1)

    def edge_cells(ref, p, q):
        gap = jnp.zeros((T, C), BF16)
        sides = [v for j in (q, 7 + q) for v in (gap, flat(ref[1 + p:7 + p, j]), gap)]
        return jnp.concatenate([flat(ref[p, q:q + 8]), flat(ref[7 + p, q:q + 8])] + sides, axis=0)

    conv_centre(pad2, w2_ref, pre2)

    def second_act(region):
        v = pre2[region]
        s = logistic(v)
        hid2[region] = (v * s).astype(BF16)
        slope_pad[moved(region, 2)] = (back2[region] * (s * (1.0 + v * (1.0 - s)))).astype(BF16)

    second_act(INSIDE)
    for tap, (p, q) in enumerate(TAPS):
        part = flip(edge_cells(pad1, p, q))
        for at in range(0, C, 64):
            row = tap * C + at
            patch_t[row // 576, row % 576:row % 576 + 64] = part[at:at + 64]
    cot_t[...] = flip(cot_p[...])
    for tap in range(9):
        at = slice(tap * C, tap * C + C)
        w1t[at] = flip(w1_ref[at])
    row_e = jnp.transpose(jnp.broadcast_to(col_e, (512, 128)))[0:1]
    row_c = jnp.transpose(jnp.broadcast_to(col_c, (128, 128)))[0:1]
    rt_mat[...] = hot(sub_f == row_e)
    rct_mat[...] = hot(sub_f[:128] == row_c)
    gt_mat[...] = hot(sub_f[:512] == te)
    gct_mat[...] = hot(sub_f[:512] == tc)

    def return_rims(n, wt):
        rows = []
        for row, p in ((2, 0), (9, 2)):
            lhs = jnp.concatenate([flat(slope_pad[row, 2 - q:12 - q]) for q in range(3)], axis=1)
            rows.append(mm(lhs, wt[3 * p * C:(3 * p + 3) * C]).astype(BF16))
        cols = []
        for col, q in ((2, 0), (9, 2)):
            part = None
            for p in range(3):
                at = slice((3 * p + q) * C, (3 * p + q + 1) * C)
                one = mm(flat(slope_pad[3 - p:11 - p, col]), wt[at])
                part = one if part is None else part + one
            cols.append(part.astype(BF16))
        top, bottom = rows
        left, right = cols
        edges = jnp.concatenate([top[T:9 * T], right, bottom[T:9 * T], left], axis=0)
        corners = jnp.concatenate(
            [top[9 * T:], bottom[9 * T:], bottom[:T], top[:T], jnp.zeros((64, C), BF16)], axis=0
        )
        pack(n, mm(rt_mat[...], edges), mm(rct_mat[...], corners))

    def back_centre(wt):
        for a in range(1, 9, 2):
            v = taps_sum(lambda p, q: flat(slope_pad[a + 2 - p:a + 4 - p, 3 - q:11 - q]), wt)
            inner[a - 1:a + 1] = v.reshape(2, S, T, C)

    def add_returned(n):
        edges, corners = ex_wait(n)
        lines = mm(gt_mat[...], edges) + mm(gct_mat[...], corners)
        lines = lines.reshape(4, S, T, C)
        inner[0] = inner[0] + lines[0]
        inner[7] = inner[7] + lines[1]
        inner[:, 0] = inner[:, 0] + lines[2]
        inner[:, 7] = inner[:, 7] + lines[3]

    fill_rims(1, pad2)
    rim_taps(pad2, w2_ref, pre2)
    for region in EDGE_LINES:
        second_act(region)
    return_rims(2, w2t)
    ex_start(2)

    hid = hid2[...].reshape(4, 2, 4, 2, T, C)

    def hid_tap(tap):
        return flat(hid[:, tap // 2, :, tap % 2])

    def put(gf, tap, per_half, at, value):
        value = jnp.transpose(value).reshape(8, 16, C)
        low = tap * 8
        for half in range(2):
            lo, hi = max(low, half * per_half), min(low + 8, (half + 1) * per_half)
            if lo < hi:
                to = slice(at + lo - half * per_half, at + hi - half * per_half)
                gf[half, to] = value[lo - low:hi - low]

    def weight_grad(slope_rows, read, gf):
        slope_t = flip(slope_rows)
        for a in range(0, 9, 2):
            taps = TAPS[a:a + 2]
            rhs = [read(p, q) for p, q in taps]
            rhs = rhs[0] if len(rhs) == 1 else jnp.concatenate(rhs, axis=1)
            both = mm(slope_t, rhs)
            for j in range(len(taps)):
                put(gf, a + j, 36, 0, both[:, j * C:(j + 1) * C])

    for tap in range(4):
        put(gf0, tap, 16, 36, mm(cot_t[...], hid_tap(tap)))
    weight_grad(
        flat(slope_pad[2:10, 2:10]), lambda p, q: flat(pad2[p:p + 8, q:q + 8]), gf0
    )

    late = ((gf0, s_a0, r_a0, r_c0), (gf1, s_a1, r_a1, r_c1))

    def owned(n, tile):
        nb = BLOCKS[n]
        b = lax.div(tile * nb + N_TILE - 1, N_TILE)
        return b, lax.div(b * N_TILE, nb) == tile

    def to_other_core(n, src_ref, dst_ref, stage):
        return pltpu.make_async_remote_copy(
            src_ref=src_ref, dst_ref=dst_ref,
            send_sem=red_send.at[n, stage], recv_sem=red_recv.at[n, stage],
            device_id=(dp, me + 1 - 2 * core), device_id_type=MESH,
        )

    def many(n, stage, count):
        at = pl.ds(0, count)
        return to_other_core(n, s_b.at[n, at], r_b.at[n, at], stage)

    def swap(n):
        return to_other_core(n, late[n][1], late[n][2], 0)

    def scatter_start(n):
        gf, _, r_a, _ = late[n]
        swap(n).wait_recv()
        s_b[n, 0:BLOCKS[n]] = (gf[core] * GRAD_SCALE + r_a[...].astype(F32)).astype(BF16)
        for rel in OFFSETS:
            tile = peer(rel)
            b, owns = owned(n, tile)
            if rel == (0, 0, 0, 0):
                @pl.when(jnp.logical_and(owns, dp == core))
                def _():
                    r_b[n, chip] = s_b[n, b]

                owns = jnp.logical_and(owns, dp != core)

            @pl.when(owns)
            def _():
                pltpu.make_async_remote_copy(
                    src_ref=s_b.at[n, b], dst_ref=r_b.at[n, chip],
                    send_sem=red_send.at[n, 1], recv_sem=red_recv.at[n, 1],
                    device_id=(core, tile), device_id_type=MESH,
                ).start()

    def share_start(n):
        b, owns = owned(n, me)

        @pl.when(owns)
        def _():
            @pl.when(dp == core)
            def _():
                many(n, 1, 63).wait_recv()

            @pl.when(dp != core)
            def _():
                many(n, 1, 64).wait_recv()

            s_c[n] = jnp.sum(r_b[n].astype(F32), axis=0).astype(BF16)
            for rel in PEERS:
                pltpu.make_async_remote_copy(
                    src_ref=s_c.at[n], dst_ref=late[n][3].at[b],
                    send_sem=red_send.at[n, 2], recv_sem=red_recv.at[n, 2],
                    device_id=(dp, peer(rel)), device_id_type=MESH,
                ).start()
            late[n][3][b] = s_c[n]

    def share_wait(n):
        b, owns = owned(n, me)

        @pl.when(owns)
        def _():
            many(n, 2, BLOCKS[n] - 1).wait_recv()

        @pl.when(jnp.logical_not(owns))
        def _():
            many(n, 2, BLOCKS[n]).wait_recv()

    s_a0[...] = (gf0[1 - core] * GRAD_SCALE).astype(BF16)
    swap(0).start()
    back_centre(w2t)
    scatter_start(0)
    feats = None
    for tap in range(4):
        part = mm(hid_tap(tap), wd_ref[tap * C:tap * C + C])
        feats = part if feats is None else feats + part
    feat_ref[...] = feats

    def first_slope(region):
        slope_pad[moved(region, 2)] = (inner[region] * silu_slope(pre1[region])).astype(BF16)

    first_slope(INSIDE)
    weight_grad(
        flat(slope_pad[3:9, 3:9]), lambda p, q: flat(pad1[1 + p:7 + p, 1 + q:7 + q]), gf1
    )

    add_returned(2)
    for region in EDGE_LINES:
        first_slope(region)
    edge_slopes = edge_cells(slope_pad, 2, 2)

    def first_grad(half):
        return gf1[half] + mm(patch_t[half], edge_slopes).reshape(36, 16, C)

    s_a1[...] = (first_grad(1 - core) * GRAD_SCALE).astype(BF16)
    swap(1).start()
    return_rims(3, w1t)
    gf1[core] = first_grad(core)
    scatter_start(1)
    back_centre(w1t)
    share_start(0)
    ex_start(3)
    share_start(1)
    add_returned(3)
    ig_ref[...] = flat(inner[...])
    share_wait(0)
    late0_ref[...] = r_c0[...]
    share_wait(1)
    late1_ref[...] = r_c1[...]

    for n in range(4):
        for copy in ex_all(n):
            copy.wait_send()
    for n in range(2):
        nb = BLOCKS[n]
        swap(n).wait_send()
        b, owns = owned(n, me)
        kept = jnp.logical_and(owns, dp == core)

        @pl.when(kept)
        def _():
            many(n, 1, nb - 1).wait_send()

        @pl.when(jnp.logical_not(kept))
        def _():
            many(n, 1, nb).wait_send()

        @pl.when(owns)
        def _():
            many(n, 2, N_TILE - 1).wait_send()


def finish(
    feat_in, ig_in, late0, late1, feat_hbm, ig_hbm, o1_hbm, o2_hbm, od_hbm,
    feat_ref, ig_ref, o1_ref, o2_ref, od_ref, sem,
):
    copies = []

    def send(src_ref, dst_ref):
        copies.append(pltpu.make_async_copy(src_ref, dst_ref, sem.at[len(copies)]))
        copies[-1].start()

    o2_ref[...] = flat(late0[0:36].astype(F32))
    send(o2_ref, o2_hbm)
    o1_ref[...] = flat(late1[...].astype(F32))
    send(o1_ref, o1_hbm)
    for t in range(T):
        ig_ref[pl.ds(t * 64, 64), :] = ig_in[pl.ds(t, 64, stride=T), :]
        if t % 4 == 3:
            part = pl.ds((t - 3) * 64, 256)
            send(ig_ref.at[part], ig_hbm.at[part])
    for t in range(T):
        feat_ref[pl.ds(t * 16, 16), :] = feat_in[pl.ds(t, 16, stride=T), :].astype(BF16)
    send(feat_ref, feat_hbm)
    od_ref[...] = flat(late0[36:52].astype(F32))
    send(od_ref, od_hbm)
    for copy in copies:
        copy.wait()


def local(inputs, cotangent, w_first, w_second, w_down, edge_owner, corner_owner, neighbour_tile, seam_rotation):
    vmem = pl.BlockSpec(memory_space=pltpu.VMEM)
    v = pltpu.VMEM
    shape = jax.ShapeDtypeStruct
    between = pl.pallas_call(
        kernel,
        out_shape=(
            shape((256, C), F32), shape((1024, C), F32), shape((52, 16, C), BF16), shape((36, 16, C), BF16),
        ),
        in_specs=[pl.BlockSpec(memory_space=pltpu.HBM)] * 9,
        out_specs=(vmem,) * 4,
        scratch_shapes=[
            v((1024, C), BF16),
            v((256, C), BF16),
            v((1152, C), BF16),
            v((1152, C), BF16),
            v((512, C), BF16),
            v((4, 1024), jnp.int32),
            v((4, 1024), jnp.int32),
            v((8, 1024), jnp.int32),
            v((8, 1024), jnp.int32),
            v((1024, C), F32),
            v((S, S, T, C), F32),
            v((S, S, T, C), F32),
            v((S, S, T, C), F32),
            v((10, 10, T, C), BF16),
            v((10, 10, T, C), BF16),
            v((12, 12, T, C), BF16),
            v((1024, 512), BF16),
            v((512, 1024), BF16),
            v((128, 512), BF16),
            v((512, 128), BF16),
            v((512, 1024), BF16),
            v((1024, 512), BF16),
            v((128, 128), BF16),
            v((128, 128), BF16),
            v((1152, C), BF16),
            v((1152, C), BF16),
            v((512, C), BF16),
            v((4, 2, 4, 2, T, C), F32),
            v((S, S, T, C), F32),
            v((S, S, T, C), BF16),
            v((256, C), BF16),
            v((C, 256), BF16),
            v((256, C), F32),
            v((2, 576, 512), BF16),
            v((2, 52, 16, C), F32),
            v((2, 36, 16, C), F32),
            v((52, 16, C), BF16),
            v((36, 16, C), BF16),
            v((52, 16, C), BF16),
            v((36, 16, C), BF16),
            v((2, 64, 16, C), BF16),
            v((2, 64, 16, C), BF16),
            v((2, 16, C), BF16),
            v((52, 16, C), BF16),
            v((36, 16, C), BF16),
            v((4, N_TILE, T, C), BF16),
            v((4, N_TILE, T, C), BF16),
            v((4, N_TILE, 2, C), BF16),
            v((4, N_TILE, 2, C), BF16),
            pltpu.SemaphoreType.DMA((9,)),
            pltpu.SemaphoreType.DMA((4, 2)),
            pltpu.SemaphoreType.DMA((4, 2)),
            pltpu.SemaphoreType.DMA((2, 3)),
            pltpu.SemaphoreType.DMA((2, 3)),
        ],
        compiler_params=pltpu.CompilerParams(
            collective_id=0, has_side_effects=True, vmem_limit_bytes=32 * 1024 * 1024
        ),
    )(
        *[
            pltpu.with_memory_space_constraint(a, pltpu.HBM)
            for a in (
                inputs.reshape(1024, C), cotangent.reshape(256, C), w_first, w_second, w_down,
                edge_owner.T, corner_owner.T, neighbour_tile.T, seam_rotation.T,
            )
        ]
    )
    feats, grads, one, two, low = pl.pallas_call(
        finish,
        out_shape=(
            shape((256, C), BF16), shape((1024, C), F32), shape((576, C), F32),
            shape((576, C), F32), shape((256, C), F32),
        ),
        in_specs=[vmem] * 4,
        out_specs=(pl.BlockSpec(memory_space=pltpu.HBM),) * 5,
        scratch_shapes=[
            v((256, C), BF16), v((1024, C), F32), v((576, C), F32), v((576, C), F32), v((256, C), F32),
            pltpu.SemaphoreType.DMA((8,)),
        ],
        compiler_params=pltpu.CompilerParams(vmem_limit_bytes=16 * 1024 * 1024),
    )(*between)
    return (feats.reshape(1, T, 4, 4, C), grads.reshape(1, T, S, S, C), one, two, low)


def solution(mesh):
    tiles = P("dp", "tile", None, None, None)
    return jax.shard_map(
        local,
        mesh=mesh,
        in_specs=(tiles, tiles) + (P(),) * 7,
        out_specs=(tiles, tiles) + (P("dp", None),) * 3,
        check_vma=False,
    )
```

```python
import itertools

import jax
import jax.numpy as jnp
import numpy as np
from jax import lax
from jax.experimental import pallas as pl
from jax.experimental.pallas import tpu as pltpu
from jax.sharding import PartitionSpec as P

MESH = pl.DeviceIdType.MESH
F32 = jnp.float32
BF16 = jnp.bfloat16
N_TILE = 64
T = 16
S = 8
C = 128
PIX = S * S * T
TAPS = [(p, q) for p in range(3) for q in range(3)]
GRAD_SCALE = float(2 * 1024 * 64) ** -0.5
BLOCKS = (36 + 16, 36)


def hops(rel):
    return min(rel[0], 4 - rel[0]) + rel[1] + min(rel[2], 4 - rel[2]) + 0.3 * rel[3]


OFFSETS = sorted(itertools.product(range(4), range(2), range(4), range(2)), key=hops, reverse=True)
PEERS = OFFSETS[:-1]
EDGE_LINES = [(0, slice(0, 8)), (7, slice(0, 8)), (slice(1, 7), 0), (slice(1, 7), 7)]
INSIDE = (slice(1, 7), slice(1, 7))


def seam_lines():
    grid = np.arange(S * S).reshape(S, S)
    sides = [grid[0], grid[-1], grid[:, 0], grid[:, -1]]
    first = np.zeros((8, 4), int)
    step = np.zeros((8, 4), int)
    for turn in range(4):
        turned = np.rot90(grid, turn)
        lines = [turned[-1, :], turned[:, 0], turned[0, :], turned[:, -1]]
        for k, line in enumerate(lines):
            for n, side in enumerate(sides):
                if (line == side).all():
                    first[k, turn], step[k, turn] = 8 * n, 1
                if (line[::-1] == side).all():
                    first[k, turn], step[k, turn] = 8 * n + 7, -1
        cells = [turned[-1, 0], turned[0, 0], turned[0, -1], turned[-1, -1]]
        for k, cell in enumerate(cells):
            first[4 + k, turn] = {0: 0, 7: 7, 56: 8, 63: 15}[int(cell)]
    return first, step


def iota(shape, axis):
    return lax.broadcasted_iota(jnp.int32, shape, axis)


def hot(mask):
    return jnp.where(mask, 1.0, 0.0).astype(BF16)


def mm(a, b):
    return jnp.dot(a, b, preferred_element_type=F32)


def mm_nt(a, b):
    return lax.dot_general(a, b, (((1,), (1,)), ((), ())), preferred_element_type=F32)


def logistic(v):
    return 1.0 / (1.0 + jnp.exp(-v))


def silu_slope(v):
    s = logistic(v)
    return s * (1.0 + v * (1.0 - s))


def flip(w):
    return jnp.transpose(w.astype(F32)).astype(BF16)


def flat(v):
    return v.reshape(-1, C)


def cells(v):
    return v.reshape(-1, T, C)


def moved(region, by):
    return tuple(slice(r.start + by, r.stop + by) if isinstance(r, slice) else r + by for r in region)


def kernel(
    x_hbm, cot_hbm, w1_hbm, w2_hbm, wd_hbm, eo_hbm, co_hbm, nb_hbm, rot_hbm,
    feat_ref, ig_ref, late0_ref, late1_ref,
    x_ref, cot_ref, w1_ref, w2_ref, wd_ref, eo_ref, co_ref, nb_ref, rot_ref,
    wide, inner, pre1, pre2, pad1, pad2, slope_pad, g_mat, gt_mat, gc_mat, gct_mat,
    r_mat, rt_mat, rc_mat, rct_mat, w1t, w2t, wdt, back6, back2, hid2, cot_p, cot_t,
    small, patch_t, gf0, gf1, s_a0, s_a1, r_a0, r_a1, s_b, r_b, s_c, r_c0, r_c1,
    s_edge, r_edge, s_corner, r_corner,
    load_sem, ex_send, ex_recv, red_send, red_recv,
):
    dp = lax.axis_index("dp")
    me = lax.axis_index("tile")
    core = lax.rem(me, 2)
    chip = dp * 32 + lax.div(me, 2)
    at_x = [lax.rem(lax.div(me, 16) + d, 4) * 16 for d in range(4)]
    at_z = [lax.rem(lax.div(me, 8) + d, 2) * 8 for d in range(2)]
    at_y = [lax.rem(lax.div(me, 2) + d, 4) * 2 for d in range(4)]
    at_c = [lax.rem(me + d, 2) for d in range(2)]

    def peer(rel):
        return at_x[rel[0]] + at_z[rel[1]] + at_y[rel[2]] + at_c[rel[3]]

    pairs = [
        (eo_hbm, eo_ref), (co_hbm, co_ref), (nb_hbm, nb_ref), (rot_hbm, rot_ref), (x_hbm, x_ref),
        (cot_hbm, cot_ref), (w1_hbm, w1_ref), (w2_hbm, w2_ref), (wd_hbm, wd_ref),
    ]
    loads = [pltpu.make_async_copy(a, b, load_sem.at[i]) for i, (a, b) in enumerate(pairs)]
    for load in loads:
        load.start()
    barrier = pltpu.get_barrier_semaphore()
    pl.semaphore_signal(barrier, inc=1, device_id=(1 - dp, me), device_id_type=MESH)
    for rel in PEERS:
        pl.semaphore_signal(barrier, inc=1, device_id=(dp, peer(rel)), device_id_type=MESH)
    for load in loads[:4]:
        load.wait()

    me_f = me.astype(F32)
    own = jnp.concatenate([eo_ref[...], co_ref[...]], axis=0).astype(F32)
    src = nb_ref[...].astype(F32)
    rot = rot_ref[...].astype(F32)
    row8 = iota((8, 1024), 0)
    first, step = seam_lines()
    base_v = jnp.zeros((8, 1024), F32)
    step_v = jnp.zeros((8, 1024), F32)
    for turn in range(4):
        bcol = jnp.zeros((8, 1024), F32)
        scol = jnp.zeros((8, 1024), F32)
        for k in range(8):
            bcol = jnp.where(row8 == k, float(first[k, turn]), bcol)
            scol = jnp.where(row8 == k, float(step[k, turn]), scol)
        base_v = jnp.where(rot == float(turn), bcol, base_v)
        step_v = jnp.where(rot == float(turn), scol, step_v)
    match = jnp.where(own == me_f, 1.0, 0.0)

    def per_kind(v):
        a = jnp.broadcast_to(jnp.sum(v[0:4], axis=0, keepdims=True), (4, 1024))
        b = jnp.broadcast_to(jnp.sum(v[4:8], axis=0, keepdims=True), (4, 1024))
        return jnp.concatenate([a, b], axis=0)

    has = per_kind(match)
    lane16 = jnp.bitwise_and(iota((8, 1024), 1), 15)
    acc = has
    for sh in (1, 2, 4, 8):
        acc = acc + jnp.where(lane16 >= sh, pltpu.roll(acc, sh, 1), 0.0)
    rank = acc - has
    table = []
    for s in range(2):
        sel = match * jnp.where(rank == float(s), 1.0, 0.0)
        for v in (sel, sel * base_v, sel * step_v, sel * src):
            table.append(per_kind(v))
    tab = jnp.concatenate([v[0:1] for v in table] + [v[4:5] for v in table], axis=0).astype(BF16)
    lane_i = iota((1, 1024), 1)
    sub_i = iota((1024, 1), 0)
    lane_f = lane_i.astype(F32)
    sub_f = sub_i.astype(F32)
    blk_l = jnp.right_shift(lane_i, 4).astype(F32)
    blk_s = jnp.right_shift(sub_i, 4).astype(F32)
    block_diag = hot(blk_s == blk_l)
    slots_e = mm(tab, block_diag)
    pair_s = jnp.right_shift(iota((128, 1), 0), 1).astype(F32)
    slots_c = mm_nt(tab, hot(pair_s == blk_l))

    def target(rows, which, px):
        v0, b0, t0, n0, v1, b1, t1, n1 = [rows[i:i + 1] for i in range(8)]
        late = which > 0.5
        valid = jnp.where(late, v1, v0)
        line = jnp.where(late, b1, b0) + jnp.where(late, t1, t0) * px
        return jnp.where(valid > 0.5, line * float(T) + jnp.where(late, n1, n0), -1.0)

    which_e = jnp.bitwise_and(jnp.right_shift(lane_i, 3), 1).astype(F32)
    place_e = jnp.bitwise_and(lane_i, 7).astype(F32)
    which_c = jnp.bitwise_and(lane_i[:, :128], 1).astype(F32)
    te = target(slots_e[0:8], which_e, place_e)
    tc = target(slots_c[8:16], which_c, 0.0)

    def as_column(row, n):
        return jnp.transpose(jnp.broadcast_to(row, (128, n)))[:, 0:1]

    to_e = jnp.zeros((1, 1024), F32)
    to_c = jnp.zeros((1, 128), F32)
    for o, rel in enumerate(OFFSETS):
        ident = peer(rel).astype(F32)
        to_e = jnp.where(blk_l == float(o), ident, to_e)
        to_c = jnp.where(jnp.right_shift(lane_i[:, :128], 1).astype(F32) == float(o), ident, to_c)
    out_e = mm(tab, hot(blk_s == to_e))
    out_c = mm_nt(tab, hot(as_column(to_c, 128) == blk_l))
    g_mat[...] = hot(as_column(target(out_e[0:8], which_e, place_e), 1024) == lane_f[:, :512])
    gc_mat[...] = hot(as_column(target(out_c[8:16], which_c, 0.0), 128) == lane_f[:, :512])

    pad1[...] = jnp.zeros_like(pad1)
    loads[4].wait()
    wide[...] = x_ref[...].astype(F32)
    for px in range(S * S):
        pad1[1 + px // S, 1 + px % S] = wide[pl.ds(px, T, stride=S * S), :].astype(BF16)

    def pack_send(n, big, edges, little, corners, send):
        s_corner[n] = mm(little[...], corners).astype(BF16).reshape(N_TILE, 2, C)
        for part in range(2):
            rows = mm(big[part * 512:part * 512 + 512], edges)
            s_edge[n, part * 32:part * 32 + 32] = rows.astype(BF16).reshape(32, T, C)
            if send:
                ex_start(n, part)

    def gather(n, pad, send):
        lines = [pad[1, 1:9], pad[8, 1:9], pad[1:9, 1], pad[1:9, 8]]
        lines = jnp.concatenate([flat(v) for v in lines], axis=0)
        pack_send(n, g_mat, lines, gc_mat, lines, send)

    def ex_copies(n, src_at, dst_at, d):
        e = pltpu.make_async_remote_copy(
            src_ref=s_edge.at[n, src_at], dst_ref=r_edge.at[n, dst_at],
            send_sem=ex_send.at[n, 0], recv_sem=ex_recv.at[n, 0],
            device_id=(dp, d), device_id_type=MESH,
        )
        c = pltpu.make_async_remote_copy(
            src_ref=s_corner.at[n, src_at], dst_ref=r_corner.at[n, dst_at],
            send_sem=ex_send.at[n, 1], recv_sem=ex_recv.at[n, 1],
            device_id=(dp, d), device_id_type=MESH,
        )
        return e, c

    def ex_start(n, part):
        for o in range(part * 32, min(part * 32 + 32, N_TILE - 1)):
            d = peer(OFFSETS[o])
            for copy in ex_copies(n, o, me, d):
                copy.start()
        if part == 1:
            r_edge[n, me] = s_edge[n, N_TILE - 1]
            r_corner[n, me] = s_corner[n, N_TILE - 1]

    def ex_all(n):
        rest = pl.ds(0, N_TILE - 1)
        return ex_copies(n, rest, rest, peer(OFFSETS[0]))

    def ex_wait(n):
        for copy in ex_all(n):
            copy.wait_recv()
        return flat(r_edge[n]), flat(r_corner[n])

    gather(0, pad1, send=False)
    pl.semaphore_wait(barrier, N_TILE)
    ex_start(0, 0)
    ex_start(0, 1)

    for load in loads[5:]:
        load.wait()
    ownb = own.astype(BF16)
    pick = hot(iota((128, 1), 0).astype(F32) + me_f * float(T) == lane_f)
    my_row = mm_nt(ownb, pick)
    my_col = mm_nt(pick[0:16], ownb)
    earlier = iota((T, 128), 1).astype(F32) < iota((T, 128), 0).astype(F32)

    def slot_base(kind, per_owner, per_rank):
        out = []
        for k in range(4 * kind, 4 * kind + 4):
            col = my_col[:, k:k + 1]
            shared = jnp.zeros((T, 128), F32)
            for k2 in range(4 * kind, 4 * kind + 4):
                shared = shared + jnp.where(col == my_row[k2:k2 + 1], 1.0, 0.0)
            rk = jnp.sum(jnp.where(earlier, shared, 0.0), axis=1, keepdims=True)
            out.append(col * per_owner + rk * per_rank)
        return out

    base_e = slot_base(0, 16.0, 8.0)
    base_c = slot_base(1, 2.0, 1.0)
    col_e = jnp.concatenate([b + float(px) for b in base_e for px in range(S)], axis=0)
    col_c = jnp.concatenate(base_c + [jnp.full((64, 1), -1.0, F32)], axis=0)
    r_mat[...] = hot(col_e == lane_f)
    rc_mat[...] = hot(col_c == lane_f[:, :128])

    def taps_sum(read, w):
        out = None
        for a in range(0, 9, 2):
            taps = TAPS[a:a + 2]
            lhs = [read(p, q) for p, q in taps]
            lhs = lhs[0] if len(lhs) == 1 else jnp.concatenate(lhs, axis=1)
            part = mm(lhs, w[a * C:(a + len(taps)) * C])
            out = part if out is None else out + part
        return out

    def conv_centre(pad, w, pre):
        for i in range(0, S, 2):
            v = taps_sum(lambda p, q: flat(pad[i + p:i + p + 2, q:q + 8]), w)
            pre[i:i + 2] = v.reshape(2, S, T, C)

    def first_act(region):
        v = pre1[region]
        pad2[moved(region, 1)] = (v * logistic(v)).astype(BF16)

    pad2[...] = jnp.zeros_like(pad2)
    slope_pad[...] = jnp.zeros_like(slope_pad)
    conv_centre(pad1, w1_ref, pre1)
    first_act(INSIDE)
    for tap in range(4):
        at = slice(tap * C, tap * C + C)
        wdt[at] = flip(wd_ref[at])
    small[...] = cot_ref[...].astype(F32)
    for px in range(16):
        cot_p[pl.ds(px * T, T), :] = small[pl.ds(px, T, stride=16), :].astype(BF16)
    for tap in range(4):
        back = mm(cot_p[...], wdt[tap * C:tap * C + C]).reshape(4, 4, T, C)
        back6[:, tap // 2, :, tap % 2] = back
    back2[...] = back6[...].reshape(S, S, T, C)
    for tap in range(9):
        at = slice(tap * C, tap * C + C)
        w2t[at] = flip(w2_ref[at])

    def fill_rims(n, pad):
        edges, corners = ex_wait(n)
        rims = mm(r_mat[...], edges).astype(BF16).reshape(4, S, T, C)
        at_corner = mm(rc_mat[...], corners).astype(BF16)
        pad[0, 1:9] = rims[0]
        pad[1:9, 9] = rims[1]
        pad[9, 1:9] = rims[2]
        pad[1:9, 0] = rims[3]
        pad[0, 9] = at_corner[0:16]
        pad[9, 9] = at_corner[16:32]
        pad[9, 0] = at_corner[32:48]
        pad[0, 0] = at_corner[48:64]

    def rim_taps(pad, w, pre):
        for i, row, p in ((0, 0, 0), (7, 9, 2)):
            lhs = jnp.concatenate([flat(pad[row, q:q + 8]) for q in range(3)], axis=1)
            pre[i] = pre[i] + cells(mm(lhs, w[3 * p * C:(3 * p + 3) * C]))
        zero = jnp.zeros((T, C), BF16)
        for j, col, q in ((0, 0, 0), (7, 9, 2)):
            lhs = [
                jnp.concatenate([zero, flat(pad[1:8, col])], axis=0),
                flat(pad[1:9, col]),
                jnp.concatenate([flat(pad[2:9, col]), zero], axis=0),
            ]
            part = None
            for p in range(3):
                one = mm(lhs[p], w[(3 * p + q) * C:(3 * p + q + 1) * C])
                part = one if part is None else part + one
            pre[:, j] = pre[:, j] + cells(part)

    fill_rims(0, pad1)
    rim_taps(pad1, w1_ref, pre1)
    for region in EDGE_LINES:
        first_act(region)
    gather(1, pad2, send=True)

    def edge_cells(ref, p, q):
        gap = jnp.zeros((T, C), BF16)
        sides = [v for j in (q, 7 + q) for v in (gap, flat(ref[1 + p:7 + p, j]), gap)]
        return jnp.concatenate([flat(ref[p, q:q + 8]), flat(ref[7 + p, q:q + 8])] + sides, axis=0)

    conv_centre(pad2, w2_ref, pre2)

    def second_act(region):
        v = pre2[region]
        s = logistic(v)
        hid2[region] = (v * s).astype(BF16)
        slope_pad[moved(region, 2)] = (back2[region] * (s * (1.0 + v * (1.0 - s)))).astype(BF16)

    second_act(INSIDE)
    for tap, (p, q) in enumerate(TAPS):
        part = flip(edge_cells(pad1, p, q))
        for at in range(0, C, 64):
            row = tap * C + at
            patch_t[row // 576, row % 576:row % 576 + 64] = part[at:at + 64]
    cot_t[...] = flip(cot_p[...])
    for tap in range(9):
        at = slice(tap * C, tap * C + C)
        w1t[at] = flip(w1_ref[at])
    row_e = jnp.transpose(jnp.broadcast_to(col_e, (512, 128)))[0:1]
    row_c = jnp.transpose(jnp.broadcast_to(col_c, (128, 128)))[0:1]
    slot_e = to_e * 16.0 + jnp.bitwise_and(lane_i, 15).astype(F32)
    rt_mat[...] = hot(as_column(slot_e, 1024) == row_e)
    rct_mat[...] = hot(as_column(to_c * 2.0 + which_c, 128) == row_c)
    gt_mat[...] = hot(sub_f[:512] == te)
    gct_mat[...] = hot(sub_f[:512] == tc)

    def return_rims(n, wt, send):
        rows = []
        for row, p in ((2, 0), (9, 2)):
            lhs = jnp.concatenate([flat(slope_pad[row, 2 - q:12 - q]) for q in range(3)], axis=1)
            rows.append(mm(lhs, wt[3 * p * C:(3 * p + 3) * C]).astype(BF16))
        cols = []
        for col, q in ((2, 0), (9, 2)):
            part = None
            for p in range(3):
                at = slice((3 * p + q) * C, (3 * p + q + 1) * C)
                one = mm(flat(slope_pad[3 - p:11 - p, col]), wt[at])
                part = one if part is None else part + one
            cols.append(part.astype(BF16))
        top, bottom = rows
        left, right = cols
        edges = jnp.concatenate([top[T:9 * T], right, bottom[T:9 * T], left], axis=0)
        corners = jnp.concatenate(
            [top[9 * T:], bottom[9 * T:], bottom[:T], top[:T], jnp.zeros((64, C), BF16)], axis=0
        )
        pack_send(n, rt_mat, edges, rct_mat, corners, send)

    def back_centre(wt):
        for a in range(1, 9, 2):
            v = taps_sum(lambda p, q: flat(slope_pad[a + 2 - p:a + 4 - p, 3 - q:11 - q]), wt)
            inner[a - 1:a + 1] = v.reshape(2, S, T, C)

    def add_returned(n):
        edges, corners = ex_wait(n)
        lines = mm(gt_mat[...], edges) + mm(gct_mat[...], corners)
        lines = lines.reshape(4, S, T, C)
        inner[0] = inner[0] + lines[0]
        inner[7] = inner[7] + lines[1]
        inner[:, 0] = inner[:, 0] + lines[2]
        inner[:, 7] = inner[:, 7] + lines[3]

    fill_rims(1, pad2)
    rim_taps(pad2, w2_ref, pre2)
    for region in EDGE_LINES:
        second_act(region)
    return_rims(2, w2t, send=True)

    hid = hid2[...].reshape(4, 2, 4, 2, T, C)

    def hid_tap(tap):
        return flat(hid[:, tap // 2, :, tap % 2])

    def put(gf, tap, per_half, at, value):
        value = jnp.transpose(value).reshape(8, 16, C)
        low = tap * 8
        for half in range(2):
            lo, hi = max(low, half * per_half), min(low + 8, (half + 1) * per_half)
            if lo < hi:
                to = slice(at + lo - half * per_half, at + hi - half * per_half)
                gf[half, to] = value[lo - low:hi - low]

    def weight_grad(slope_rows, read, gf):
        slope_t = flip(slope_rows)
        for a in range(0, 9, 2):
            taps = TAPS[a:a + 2]
            rhs = [read(p, q) for p, q in taps]
            rhs = rhs[0] if len(rhs) == 1 else jnp.concatenate(rhs, axis=1)
            both = mm(slope_t, rhs)
            for j in range(len(taps)):
                put(gf, a + j, 36, 0, both[:, j * C:(j + 1) * C])

    for tap in range(4):
        put(gf0, tap, 16, 36, mm(cot_t[...], hid_tap(tap)))
    weight_grad(
        flat(slope_pad[2:10, 2:10]), lambda p, q: flat(pad2[p:p + 8, q:q + 8]), gf0
    )

    late = ((gf0, s_a0, r_a0, r_c0), (gf1, s_a1, r_a1, r_c1))

    def owned(n, tile):
        nb = BLOCKS[n]
        b = lax.div(tile * nb + N_TILE - 1, N_TILE)
        return b, lax.div(b * N_TILE, nb) == tile

    def to_other_core(n, src_ref, dst_ref, stage):
        return pltpu.make_async_remote_copy(
            src_ref=src_ref, dst_ref=dst_ref,
            send_sem=red_send.at[n, stage], recv_sem=red_recv.at[n, stage],
            device_id=(dp, me + 1 - 2 * core), device_id_type=MESH,
        )

    def many(n, stage, count):
        at = pl.ds(0, count)
        return to_other_core(n, s_b.at[n, at], r_b.at[n, at], stage)

    def swap(n):
        return to_other_core(n, late[n][1], late[n][2], 0)

    def scatter_start(n):
        gf, _, r_a, _ = late[n]
        swap(n).wait_recv()
        s_b[n, 0:BLOCKS[n]] = (gf[core] * GRAD_SCALE + r_a[...].astype(F32)).astype(BF16)
        for rel in OFFSETS:
            tile = peer(rel)
            b, owns = owned(n, tile)
            if rel == (0, 0, 0, 0):
                @pl.when(jnp.logical_and(owns, dp == core))
                def _():
                    r_b[n, chip] = s_b[n, b]

                owns = jnp.logical_and(owns, dp != core)

            @pl.when(owns)
            def _():
                pltpu.make_async_remote_copy(
                    src_ref=s_b.at[n, b], dst_ref=r_b.at[n, chip],
                    send_sem=red_send.at[n, 1], recv_sem=red_recv.at[n, 1],
                    device_id=(core, tile), device_id_type=MESH,
                ).start()

    def share_start(n):
        b, owns = owned(n, me)

        @pl.when(owns)
        def _():
            @pl.when(dp == core)
            def _():
                many(n, 1, 63).wait_recv()

            @pl.when(dp != core)
            def _():
                many(n, 1, 64).wait_recv()

            s_c[n] = jnp.sum(r_b[n].astype(F32), axis=0).astype(BF16)
            for rel in PEERS:
                pltpu.make_async_remote_copy(
                    src_ref=s_c.at[n], dst_ref=late[n][3].at[b],
                    send_sem=red_send.at[n, 2], recv_sem=red_recv.at[n, 2],
                    device_id=(dp, peer(rel)), device_id_type=MESH,
                ).start()
            late[n][3][b] = s_c[n]

    def share_wait(n):
        b, owns = owned(n, me)

        @pl.when(owns)
        def _():
            many(n, 2, BLOCKS[n] - 1).wait_recv()

        @pl.when(jnp.logical_not(owns))
        def _():
            many(n, 2, BLOCKS[n]).wait_recv()

    s_a0[...] = (gf0[1 - core] * GRAD_SCALE).astype(BF16)
    swap(0).start()
    back_centre(w2t)
    scatter_start(0)
    feats = None
    for tap in range(4):
        part = mm(hid_tap(tap), wd_ref[tap * C:tap * C + C])
        feats = part if feats is None else feats + part
    feat_ref[...] = feats

    def first_slope(region):
        slope_pad[moved(region, 2)] = (inner[region] * silu_slope(pre1[region])).astype(BF16)

    first_slope(INSIDE)
    weight_grad(
        flat(slope_pad[3:9, 3:9]), lambda p, q: flat(pad1[1 + p:7 + p, 1 + q:7 + q]), gf1
    )

    add_returned(2)
    for region in EDGE_LINES:
        first_slope(region)
    edge_slopes = edge_cells(slope_pad, 2, 2)

    def first_grad(half):
        return gf1[half] + mm(patch_t[half], edge_slopes).reshape(36, 16, C)

    s_a1[...] = (first_grad(1 - core) * GRAD_SCALE).astype(BF16)
    swap(1).start()
    return_rims(3, w1t, send=False)
    gf1[core] = first_grad(core)
    scatter_start(1)
    back_centre(w1t)
    share_start(0)
    ex_start(3, 0)
    ex_start(3, 1)
    share_start(1)
    add_returned(3)
    ig_ref[...] = flat(inner[...])
    share_wait(0)
    late0_ref[...] = r_c0[...]
    share_wait(1)
    late1_ref[...] = r_c1[...]

    for n in range(4):
        for copy in ex_all(n):
            copy.wait_send()
    for n in range(2):
        nb = BLOCKS[n]
        swap(n).wait_send()
        b, owns = owned(n, me)
        kept = jnp.logical_and(owns, dp == core)

        @pl.when(kept)
        def _():
            many(n, 1, nb - 1).wait_send()

        @pl.when(jnp.logical_not(kept))
        def _():
            many(n, 1, nb).wait_send()

        @pl.when(owns)
        def _():
            many(n, 2, N_TILE - 1).wait_send()


def finish(
    feat_in, ig_in, late0, late1, feat_hbm, ig_hbm, o1_hbm, o2_hbm, od_hbm,
    feat_ref, ig_ref, o1_ref, o2_ref, od_ref, sem,
):
    copies = []

    def send(src_ref, dst_ref):
        copies.append(pltpu.make_async_copy(src_ref, dst_ref, sem.at[len(copies)]))
        copies[-1].start()

    o2_ref[...] = flat(late0[0:36].astype(F32))
    send(o2_ref, o2_hbm)
    o1_ref[...] = flat(late1[...].astype(F32))
    send(o1_ref, o1_hbm)
    for t in range(T):
        ig_ref[pl.ds(t * 64, 64), :] = ig_in[pl.ds(t, 64, stride=T), :]
        if t % 4 == 3:
            part = pl.ds((t - 3) * 64, 256)
            send(ig_ref.at[part], ig_hbm.at[part])
    for t in range(T):
        feat_ref[pl.ds(t * 16, 16), :] = feat_in[pl.ds(t, 16, stride=T), :].astype(BF16)
    send(feat_ref, feat_hbm)
    od_ref[...] = flat(late0[36:52].astype(F32))
    send(od_ref, od_hbm)
    for copy in copies:
        copy.wait()


def local(inputs, cotangent, w_first, w_second, w_down, edge_owner, corner_owner, neighbour_tile, seam_rotation):
    vmem = pl.BlockSpec(memory_space=pltpu.VMEM)
    v = pltpu.VMEM
    shape = jax.ShapeDtypeStruct
    between = pl.pallas_call(
        kernel,
        out_shape=(
            shape((256, C), F32), shape((1024, C), F32), shape((52, 16, C), BF16), shape((36, 16, C), BF16),
        ),
        in_specs=[pl.BlockSpec(memory_space=pltpu.HBM)] * 9,
        out_specs=(vmem,) * 4,
        scratch_shapes=[
            v((1024, C), BF16),
            v((256, C), BF16),
            v((1152, C), BF16),
            v((1152, C), BF16),
            v((512, C), BF16),
            v((4, 1024), jnp.int32),
            v((4, 1024), jnp.int32),
            v((8, 1024), jnp.int32),
            v((8, 1024), jnp.int32),
            v((1024, C), F32),
            v((S, S, T, C), F32),
            v((S, S, T, C), F32),
            v((S, S, T, C), F32),
            v((10, 10, T, C), BF16),
            v((10, 10, T, C), BF16),
            v((12, 12, T, C), BF16),
            v((1024, 512), BF16),
            v((512, 1024), BF16),
            v((128, 512), BF16),
            v((512, 128), BF16),
            v((512, 1024), BF16),
            v((1024, 512), BF16),
            v((128, 128), BF16),
            v((128, 128), BF16),
            v((1152, C), BF16),
            v((1152, C), BF16),
            v((512, C), BF16),
            v((4, 2, 4, 2, T, C), F32),
            v((S, S, T, C), F32),
            v((S, S, T, C), BF16),
            v((256, C), BF16),
            v((C, 256), BF16),
            v((256, C), F32),
            v((2, 576, 512), BF16),
            v((2, 52, 16, C), F32),
            v((2, 36, 16, C), F32),
            v((52, 16, C), BF16),
            v((36, 16, C), BF16),
            v((52, 16, C), BF16),
            v((36, 16, C), BF16),
            v((2, 64, 16, C), BF16),
            v((2, 64, 16, C), BF16),
            v((2, 16, C), BF16),
            v((52, 16, C), BF16),
            v((36, 16, C), BF16),
            v((4, N_TILE, T, C), BF16),
            v((4, N_TILE, T, C), BF16),
            v((4, N_TILE, 2, C), BF16),
            v((4, N_TILE, 2, C), BF16),
            pltpu.SemaphoreType.DMA((9,)),
            pltpu.SemaphoreType.DMA((4, 2)),
            pltpu.SemaphoreType.DMA((4, 2)),
            pltpu.SemaphoreType.DMA((2, 3)),
            pltpu.SemaphoreType.DMA((2, 3)),
        ],
        compiler_params=pltpu.CompilerParams(
            collective_id=0, has_side_effects=True, vmem_limit_bytes=32 * 1024 * 1024
        ),
    )(
        *[
            pltpu.with_memory_space_constraint(a, pltpu.HBM)
            for a in (
                inputs.reshape(1024, C), cotangent.reshape(256, C), w_first, w_second, w_down,
                edge_owner.T, corner_owner.T, neighbour_tile.T, seam_rotation.T,
            )
        ]
    )
    feats, grads, one, two, low = pl.pallas_call(
        finish,
        out_shape=(
            shape((256, C), BF16), shape((1024, C), F32), shape((576, C), F32),
            shape((576, C), F32), shape((256, C), F32),
        ),
        in_specs=[vmem] * 4,
        out_specs=(pl.BlockSpec(memory_space=pltpu.HBM),) * 5,
        scratch_shapes=[
            v((256, C), BF16), v((1024, C), F32), v((576, C), F32), v((576, C), F32), v((256, C), F32),
            pltpu.SemaphoreType.DMA((8,)),
        ],
        compiler_params=pltpu.CompilerParams(vmem_limit_bytes=16 * 1024 * 1024),
    )(*between)
    return (feats.reshape(1, T, 4, 4, C), grads.reshape(1, T, S, S, C), one, two, low)


def solution(mesh):
    tiles = P("dp", "tile", None, None, None)
    return jax.shard_map(
        local,
        mesh=mesh,
        in_specs=(tiles, tiles) + (P(),) * 7,
        out_specs=(tiles, tiles) + (P("dp", None),) * 3,
        check_vma=False,
    )
```
